32 devices in a mesh: gx: 16 (over z, y, core), gy: 2 (over x).
Axes of the slice: x: 2, y: 2, z: 4, core: 2. Of those that a mesh axis runs over, the one named last changes fastest.
Arguments:
- prior_members: float32 [64, 3, 2, 128, 256], P(None, None, None, 'gx', 'gy'), may hold values from -0.25 to 0.25
- obs_column: int32 [16, 2, 256], P('gx', 'gy'), may hold values from 0 to 1023
- obs_value: float32 [16, 2, 256], P('gx', 'gy'), may hold values from -0.3 to 0.3
- obs_precision: float32 [16, 2, 256], P('gx', 'gy'), may hold values from 20 to 400
- obs_list: int32 [16, 32, 128], P('gx', 'gy'), may hold values from 0 to 2303, as said below
- patch_count: int32 [16, 32], P('gx', 'gy'), may hold values from 1 to 128, as said below
Outputs:
- analysis: float32 [64, 3, 2, 128, 256], P(None, None, None, 'gx', 'gy')
The draws below stay inside these ranges and needn't reach their ends.
Inputs may be any that keep to these rules, and one draw needn't show every extreme that they name: `obs_list`: entry e of a patch's list names slot e % 256 of the tile displaced by (e // 256 // 3 - 1, e // 256 % 3 - 1) tiles in (longitude, latitude) from the patch's own tile, longitude wrapping around; never a tile beyond the latitude edges. Entries at and past the patch's count are ignored. `patch_count`: counts differ strongly from tile to tile.
All inputs are finite; a program needn't handle non-finite values.
Results may differ from the reference program's by a relative error of at most 0.0003.
Values sent between devices are 32-bit elements; how exact they have to be, the bound alone decides.
A program may use at most 64 MiB of HBM per device.

```python
import math
import jax
import jax.numpy as jnp
from jax import lax

K = 64
LEV = 2
CX = 8
CY = 128
TILE_WIDTH_CELLS = 8
STEPS = 3
OBS_DEV = 256
OBSERVATION_CAP = 128
NS_ITERS = 3
TILES_X = 16
TILES_Y = 2
NX = 128
NY = 256
PX = 16
PY = 32


def observation_plan(key):
    base_key = jax.random.fold_in(key, 417)
    subkeys = jax.random.split(base_key, 6)
    raw_counts = jax.random.randint(subkeys[0], (TILES_X, TILES_Y), 0, OBS_DEV + 1)
    tile_counts = jnp.maximum(1, raw_counts * raw_counts // OBS_DEV)
    busiest = jax.random.randint(subkeys[1], (), 0, TILES_X * TILES_Y)
    flat_counts = tile_counts.reshape(-1)
    flat_counts = jnp.where(jnp.arange(TILES_X * TILES_Y) == busiest, OBS_DEV, flat_counts)
    tile_counts = flat_counts.reshape(TILES_X, TILES_Y)
    per_row = CX // TILE_WIDTH_CELLS
    per_col = CY // TILE_WIDTH_CELLS
    home_x = jnp.arange(PX) // per_row
    home_y = jnp.arange(PY) // per_col
    own_counts = tile_counts[home_x[:, None], home_y[None, :]]
    nominal = jnp.maximum(1, OBSERVATION_CAP * own_counts // OBS_DEV)
    jitter = jax.random.randint(subkeys[2], (PX, PY), 0, 4)
    counts = jnp.maximum(1, nominal - jitter * nominal // 8)
    first_x = busiest // TILES_Y * per_row
    first_y = busiest % TILES_Y * per_col
    marked = (jnp.arange(PX)[:, None] == first_x) & (jnp.arange(PY)[None, :] == first_y)
    counts = jnp.where(marked, OBSERVATION_CAP, counts)
    shift_x = jax.random.randint(subkeys[3], (PX, PY, OBSERVATION_CAP), -1, 2)
    shift_y = jax.random.randint(subkeys[4], (PX, PY, OBSERVATION_CAP), -1, 2)
    target_y = home_y[None, :, None] + shift_y
    shift_y = jnp.where((target_y >= 0) & (target_y < TILES_Y), shift_y, 0)
    source_x = (home_x[:, None, None] + shift_x) % TILES_X
    source_y = home_y[None, :, None] + shift_y
    available = tile_counts[source_x, source_y]
    slot_index = jax.random.randint(subkeys[5], (PX, PY, OBSERVATION_CAP), 0, available)
    entries = ((shift_x + 1) * 3 + shift_y + 1) * OBS_DEV + slot_index
    return (counts.astype(jnp.int32), entries.astype(jnp.int32))


def draw_obs_list(key, part):
    return observation_plan(key)[1]


def draw_patch_count(key, part):
    return observation_plan(key)[0]


def plant(drawn, stream_key, smallest, largest):
    extent = drawn.shape
    index_at = [jax.random.randint(jax.random.fold_in(stream_key, axis), (), 0, extent[axis]) for axis in range(len(extent))]
    drawn = drawn.at[tuple(index_at)].set(smallest)
    longest = extent.index(max(extent))
    index_at[longest] = (index_at[longest] + 1) % extent[longest]
    return drawn.at[tuple(index_at)].set(largest)


def steps_of(own_key, dims, cuts, low, largest):
    def one(position, parts):
        steps = jax.random.uniform(jax.random.fold_in(jax.random.fold_in(own_key, 6), position), (parts,), jnp.float32, low / len(cuts), largest / len(cuts))
        return jnp.repeat(jnp.exp(steps), dims[position] // parts).reshape((-1,) + (1,) * (len(dims) - position - 1))

    gain = one(*cuts[0])
    for cut in cuts[1:]:
        gain = gain * one(*cut)
    return gain


def noise(rng, dims, width, most, cuts=(), held_as=jnp.bfloat16):
    drawn = width * jax.random.normal(rng, dims, jnp.float32)
    if cuts:
        drawn = drawn * steps_of(rng, dims, cuts, -0.22, 0.18)
    return jnp.clip(drawn, -most, most).astype(held_as)


def setup_inputs(seed: int = 0) -> dict:
    splits = jax.random.split(jax.random.key(seed), 7)
    return {
        "prior_members": jnp.clip(jax.random.uniform(splits[0], (K, 3, LEV, NX, NY), jnp.float32, -0.25, 0.25) * steps_of(splits[0], (K, 3, LEV, NX, NY), ((3, 16), (4, 2)), -0.4, 0.0), -0.25, 0.25),
        "obs_column": plant(jax.random.randint(splits[1], (TILES_X, TILES_Y, OBS_DEV), 0, CX * CY), jax.random.fold_in(splits[1], 1), 0, (CX * CY) - 1).astype(jnp.int32),
        "obs_value": noise(splits[2], (TILES_X, TILES_Y, OBS_DEV), 0.05, 0.3, ((0, 16), (1, 2)), jnp.float32),
        "obs_precision": jnp.clip(jnp.exp(math.log(400.0) - 2.9957323 * jax.random.uniform(splits[3], (TILES_X, TILES_Y, OBS_DEV), jnp.float32) ** steps_of(splits[3], (TILES_X, TILES_Y, OBS_DEV), ((0, 16), (1, 2)), -0.2, 0.2)), 20.0, 400.0),
        "obs_list": draw_obs_list(jax.random.fold_in(splits[6], 71), 0),
        "patch_count": draw_patch_count(jax.random.fold_in(splits[6], 71), 0),
    }


courant = 0.3
highest = lax.Precision.HIGHEST

def friedrichs_step(padded):
    depths = 1.0 + padded[..., 0, :, :, :]
    momentum_x = padded[..., 1, :, :, :]
    momentum_y = padded[..., 2, :, :, :]
    pressure = 0.5 * depths * depths
    cross_flux = momentum_x * momentum_y / depths
    flux_x = jnp.stack([momentum_x, momentum_x * momentum_x / depths + pressure, cross_flux], axis=-4)
    flux_y = jnp.stack([momentum_y, cross_flux, momentum_y * momentum_y / depths + pressure], axis=-4)
    neighbours = padded[..., 2:, 1:-1] + padded[..., :-2, 1:-1] + padded[..., 1:-1, 2:] + padded[..., 1:-1, :-2]
    return 0.25 * neighbours - 0.5 * courant * (flux_x[..., 2:, 1:-1] - flux_x[..., :-2, 1:-1]) - 0.5 * courant * (flux_y[..., 1:-1, 2:] - flux_y[..., 1:-1, :-2])

def analyse(fields, members_obs, values, precisions, offset_x, offset_y, usable):
    members = fields.shape[1]
    obs_mean = lax.optimization_barrier(jnp.mean(members_obs, axis=1))
    obs_pert = members_obs - obs_mean[:, None, :]
    departure = values - obs_mean
    weights = usable * precisions * jnp.exp(-(offset_x / CX) ** 2 - (offset_y / CY) ** 2)
    gram_matrix = jnp.einsum('bkm,bjm->bkj', obs_pert * weights[:, None, :], obs_pert, precision=highest)
    bounds = members - 1.0 + lax.optimization_barrier(jnp.sum(weights * lax.optimization_barrier(jnp.sum(obs_pert * obs_pert, axis=1)), axis=1))
    identity = jnp.eye(members, dtype=jnp.float32)
    scaled = (gram_matrix + (members - 1.0) * identity) / bounds[:, None, None]
    iterate = scaled
    inverse_root = jnp.broadcast_to(identity, scaled.shape)
    for repeat in range(NS_ITERS):
        factor = 1.5 * identity - 0.5 * jnp.einsum('bij,bjk->bik', inverse_root, iterate, precision=highest)
        iterate = jnp.einsum('bij,bjk->bik', iterate, factor, precision=highest)
        inverse_root = jnp.einsum('bij,bjk->bik', factor, inverse_root, precision=highest)
    forcing = jnp.einsum('bkm,bm->bk', obs_pert, weights * departure, precision=highest)
    half_way = jnp.einsum('bij,bj->bi', inverse_root, forcing, precision=highest)
    mean_weight = jnp.einsum('bij,bj->bi', inverse_root, half_way, precision=highest) / bounds[:, None]
    spread_weight = jnp.sqrt((members - 1.0) / bounds)[:, None, None] * inverse_root
    combined = spread_weight + mean_weight[:, :, None]
    field_mean = lax.optimization_barrier(jnp.mean(fields, axis=1))
    field_pert = fields - field_mean[:, None, :]
    return field_mean[:, None, :] + jnp.einsum('bif,bik->bkf', field_pert, combined, precision=highest)

def integrate_dynamics(states):
    for repeat in range(STEPS):
        wrapped = jnp.concatenate([states[..., -1:, :], states, states[..., :1, :]], axis=-2)
        padded = jnp.pad(wrapped, ((0, 0), (0, 0), (0, 0), (1, 1)))
        states = friedrichs_step(padded)
    return states

def reference(prior_members, obs_column, obs_value, obs_precision, obs_list, patch_count):
    predicted_fields = lax.map(integrate_dynamics, prior_members)
    layer_mean_value = lax.optimization_barrier(jnp.mean(predicted_fields[:, 0], axis=1))
    tile_x = jnp.arange(TILES_X, dtype=jnp.int32)[:, None, None]
    tile_y = jnp.arange(TILES_Y, dtype=jnp.int32)[None, :, None]
    local_x = obs_column // CY
    local_y = obs_column % CY
    members_obs = layer_mean_value[:, tile_x * CX + local_x, tile_y * CY + local_y]
    members_obs = jnp.transpose(members_obs, (1, 2, 0, 3))
    extras = jnp.stack([obs_value, obs_precision, local_x.astype(jnp.float32), local_y.astype(jnp.float32)], axis=2)
    obs_table = jnp.concatenate([members_obs, extras], axis=2)
    per_row = CX // TILE_WIDTH_CELLS
    per_col = CY // TILE_WIDTH_CELLS
    patch_y = jnp.arange(PY, dtype=jnp.int32)
    slot_range = jnp.arange(OBSERVATION_CAP, dtype=jnp.int32)

    def row_update(latitude_index):
        latitude_strip = lax.dynamic_slice_in_dim(predicted_fields, latitude_index * TILE_WIDTH_CELLS, TILE_WIDTH_CELLS, 3)
        blocks = latitude_strip.reshape(K, 3, LEV, TILE_WIDTH_CELLS, PY, TILE_WIDTH_CELLS)
        fields = jnp.transpose(blocks, (4, 0, 1, 2, 3, 5)).reshape(PY, K, 3 * LEV * TILE_WIDTH_CELLS * TILE_WIDTH_CELLS)
        entries = obs_list[latitude_index]
        offset = entries // OBS_DEV
        slot_index = entries % OBS_DEV
        shift_x = offset // 3 - 1
        shift_y = offset % 3 - 1
        home_x = latitude_index // per_row
        home_y = patch_y // per_col
        source_x = (home_x + shift_x) % TILES_X
        source_y = jnp.clip(home_y[:, None] + shift_y, 0, TILES_Y - 1)
        picked = obs_table[source_x, source_y, :, slot_index]
        picked_obs = jnp.transpose(picked[:, :, :K], (0, 2, 1))
        centre_x = (latitude_index % per_row * TILE_WIDTH_CELLS).astype(jnp.float32) + (TILE_WIDTH_CELLS - 1) * 0.5
        centre_y = (patch_y % per_col * TILE_WIDTH_CELLS).astype(jnp.float32) + (TILE_WIDTH_CELLS - 1) * 0.5
        offset_x = (shift_x * CX).astype(jnp.float32) + picked[:, :, K + 2] - centre_x
        offset_y = (shift_y * CY).astype(jnp.float32) + picked[:, :, K + 3] - centre_y[:, None]
        usable = (slot_range[None, :] < patch_count[latitude_index][:, None]).astype(jnp.float32)
        result = analyse(fields, picked_obs, picked[:, :, K], picked[:, :, K + 1], offset_x, offset_y, usable)
        result = result.reshape(PY, K, 3, LEV, TILE_WIDTH_CELLS, TILE_WIDTH_CELLS)
        return jnp.transpose(result, (1, 2, 3, 4, 0, 5)).reshape(K, 3, LEV, TILE_WIDTH_CELLS, NY)
    row_results = lax.map(row_update, jnp.arange(PX, dtype=jnp.int32))
    return jnp.transpose(row_results, (1, 2, 3, 0, 4, 5)).reshape(K, 3, LEV, NX, NY)
```

```python
import functools

import jax
import jax.numpy as jnp
from jax import lax
from jax.experimental import pallas as pl
from jax.experimental.pallas import tpu as pltpu
from jax.sharding import PartitionSpec as P

CX = 8
CY = 128
TILE_WIDTH_CELLS = 8
STEPS = 3
NS_ITERS = 3


courant = 0.3
highest = lax.Precision.HIGHEST


def padded_2(x, sides, width):
    for axis, dim in sides:
        devices, length = (lax.axis_size(axis), x.shape[dim])
        up = [(i, (i + 1) % devices) for i in range(devices)]
        down = [(j, i) for i, j in up]
        last = lax.slice_in_dim(x, length - width, length, axis=dim)
        initial = lax.slice_in_dim(x, 0, width, axis=dim)
        before = lax.ppermute(last, axis, up)
        after = lax.ppermute(initial, axis, down)
        x = jnp.concatenate([before, x, after], axis=dim)
    return x


def friedrichs_step(padded):
    depths = 1.0 + padded[..., 0, :, :, :]
    momentum_x = padded[..., 1, :, :, :]
    momentum_y = padded[..., 2, :, :, :]
    pressure = 0.5 * depths * depths
    cross_flux = momentum_x * momentum_y / depths
    flux_x = jnp.stack(
        [momentum_x, momentum_x * momentum_x / depths + pressure, cross_flux], axis=-4
    )
    flux_y = jnp.stack(
        [momentum_y, cross_flux, momentum_y * momentum_y / depths + pressure], axis=-4
    )
    neighbours = (
        padded[..., 2:, 1:-1]
        + padded[..., :-2, 1:-1]
        + padded[..., 1:-1, 2:]
        + padded[..., 1:-1, :-2]
    )
    return (
        0.25 * neighbours
        - 0.5 * courant * (flux_x[..., 2:, 1:-1] - flux_x[..., :-2, 1:-1])
        - 0.5 * courant * (flux_y[..., 1:-1, 2:] - flux_y[..., 1:-1, :-2])
    )


def cut_outside(padded, patch_border):
    extent = padded.shape[-1] - 2 * patch_border
    global_rows = (
        lax.iota(jnp.int32, padded.shape[-1]) + lax.axis_index("gy") * extent - patch_border
    )
    inside = (global_rows >= 0) & (global_rows < extent * lax.axis_size("gy"))
    return padded * inside.astype(padded.dtype)


def split(x):
    hi = x.astype(jnp.bfloat16)
    return hi, (x - hi.astype(jnp.float32)).astype(jnp.bfloat16)


def dot_nn(a, b):
    return lax.dot_general(a, b, (((1,), (0,)), ((), ())), preferred_element_type=jnp.float32)


def dot_nt(a, b):
    return lax.dot_general(a, b, (((1,), (1,)), ((), ())), preferred_element_type=jnp.float32)


def analysis_kernel(
    geometry, fields_ref, table_ref, extras_ref, list_ref, count_ref, out_ref,
    weights, gram, force, turned, combined, result_ref, done_sem,
):
    width_x, width_y, patches_x, patches_y, rows_in_y = geometry
    kinds, columns, members, lanes = fields_ref.shape
    tiles, _, slots = extras_ref.shape
    batch, capacity = list_ref.shape
    per_tile = slots // 128
    halves = kinds * columns // 2

    chunks = tiles * per_tile
    padded_chunks = -(-chunks // 8) * 8
    usable_at = lax.broadcasted_iota(jnp.int32, (1, capacity), 1)
    chunk_id = lax.broadcasted_iota(jnp.int32, (padded_chunks, capacity), 0)
    lane_id = lax.broadcasted_iota(jnp.int32, (128, capacity), 0)
    for patch in range(batch):
        named = list_ref[patch : patch + 1, :]
        usable = usable_at < count_ref[patch : patch + 1, :]
        upper = jnp.where(usable, named // 128, -1)
        lower = named % 128
        counts = dot_nt(
            (chunk_id == upper).astype(jnp.float32).astype(jnp.bfloat16),
            (lane_id == lower).astype(jnp.float32).astype(jnp.bfloat16),
        )
        for chunk in range(chunks):
            tile, part = divmod(chunk, per_tile)
            weights[tile, patch : patch + 1, part * 128 : part * 128 + 128] = counts[
                chunk : chunk + 1
            ]

    patch_id = lax.broadcasted_iota(jnp.int32, (batch, slots), 0)
    centre_x = (patch_id // patches_y * TILE_WIDTH_CELLS).astype(jnp.float32) + (
        TILE_WIDTH_CELLS - 1
    ) * 0.5
    centre_y = (patch_id % patches_y * TILE_WIDTH_CELLS).astype(jnp.float32) + (
        TILE_WIDTH_CELLS - 1
    ) * 0.5
    gram[...] = jnp.zeros_like(gram)
    force[...] = jnp.zeros_like(force)
    for tile in range(tiles):
        shift_x, shift_y = tile // 3 - 1, tile % 3 - 1

        def add_tile():
            info = extras_ref[tile]
            offset_x = shift_x * width_x + info[2:3] - centre_x
            offset_y = shift_y * width_y + info[3:4] - centre_y
            near = jnp.exp(-((offset_x / width_x) ** 2) - (offset_y / width_y) ** 2)
            factor = weights[tile] * info[1:2] * near
            values = table_ref[tile]
            mean = jnp.sum(values, axis=0, keepdims=True) / members
            pert = values - mean
            upper, lower = split(pert)
            both = jnp.concatenate([upper, lower], axis=0)
            for patch in range(batch):
                first, second = split(pert * factor[patch : patch + 1])
                gram[patch] += dot_nt(jnp.concatenate([first, second], axis=0), both)
            first, second = split(factor * (info[0:1] - mean))
            rest = jnp.zeros((128 - 2 * batch, slots), jnp.bfloat16)
            force[...] += dot_nt(both, jnp.concatenate([first, second, rest], axis=0))

        row = lax.axis_index("gy") + shift_y
        pl.when((row >= 0) & (row < rows_in_y))(add_tile)

    for half in range(halves):
        kind, column = divmod(2 * half, columns)
        pair = []
        for step in range(2):
            block = fields_ref[kind, column + step]
            pair.append(block - jnp.sum(block, axis=0, keepdims=True) / members)
        flipped = jnp.transpose(jnp.concatenate(pair, axis=0))
        for strip in range(patches_y):
            turned[strip, half * 8 : half * 8 + 8, :] = flipped[strip * 8 : strip * 8 + 8]

    ahead = 256 // members
    groups = batch // ahead
    lane128 = lax.broadcasted_iota(jnp.int32, (members, 128), 1)
    own_row = lax.broadcasted_iota(jnp.int32, (members, 128), 0)
    diagonal = lane128 % members == own_row
    on_left = lane128 < members
    identity1 = jnp.where(diagonal, 1.0, 0.0)
    identity = jnp.concatenate([identity1, identity1], axis=1)
    in_block = (
        lax.broadcasted_iota(jnp.int32, (256, 256), 0) // members
        == lax.broadcasted_iota(jnp.int32, (256, 256), 1) // members
    ).astype(jnp.float32).astype(jnp.bfloat16)

    def tiled(part):
        return jnp.concatenate([part] * ahead, axis=0) * in_block

    def left(x):
        hi, lo = split(x)
        return jnp.concatenate([hi, lo], axis=0), hi

    def right(x):
        hi, lo = split(x)
        return tiled(hi), tiled(lo)

    def product(x, y):
        both = dot_nn(x[0], y[0])
        return both[:members] + both[members:] + dot_nn(x[1], y[1])

    scaled, inverse_bounds = [], []
    for group in range(groups):
        parts, bounds = [], []
        for pair in range(ahead // 2):
            even = gram[group * ahead + 2 * pair]
            odd = gram[group * ahead + 2 * pair + 1]
            matrix = jnp.where(
                on_left,
                even[:members] + pltpu.roll(even[:members], members, 1) + even[members:],
                odd[:members]
                + pltpu.roll(odd[:members], members, 1)
                + pltpu.roll(odd[members:], members, 1),
            )
            trace = jnp.where(diagonal, matrix, 0.0)
            first = jnp.sum(jnp.where(on_left, trace, 0.0), keepdims=True)
            second = jnp.sum(jnp.where(on_left, 0.0, trace), keepdims=True)
            bounds.append(members - 1.0 + jnp.where(on_left[:1], first, second))
            parts.append(matrix)
        bounds = jnp.concatenate(bounds, axis=1)
        matrix = jnp.concatenate(parts, axis=1)
        scaled.append((matrix + (members - 1.0) * identity) / bounds)
        inverse_bounds.append(1.0 / bounds)

    iterate = [left(a) for a in scaled]
    values = scaled
    factors = [1.5 * identity - 0.5 * a for a in scaled]
    roots = factors
    for repeat in range(1, NS_ITERS):
        factor_right = [right(s) for s in factors]
        iterate = [left(v) for v in values]
        values = [product(y, s) for y, s in zip(iterate, factor_right)]
        root_left = [left(z) for z in roots]
        value_right = [right(v) for v in values]
        factors = [
            1.5 * identity - 0.5 * product(z, y) for z, y in zip(root_left, value_right)
        ]
        factor_left = [left(s) for s in factors]
        root_right = [right(z) for z in roots]
        roots = [product(s, z) for s, z in zip(factor_left, root_right)]

    total = force[...]
    forcing = (
        total[:members] + pltpu.roll(total[:members], 128 - batch, 1) + total[members:]
    )
    block_row = lax.broadcasted_iota(jnp.int32, (256, 128), 0) // members
    block_lane = lax.broadcasted_iota(jnp.int32, (256, 128), 1)
    for group in range(groups):
        root = left(roots[group])
        keep = (block_row + group * ahead == block_lane).astype(jnp.float32).astype(jnp.bfloat16)
        vector = forcing
        for repeat in range(2):
            hi, lo = split(vector)
            hi = jnp.concatenate([hi] * ahead, axis=0) * keep
            lo = jnp.concatenate([lo] * ahead, axis=0) * keep
            vector = product(root, (hi, lo))
        shift = []
        for pair in range(ahead // 2):
            first = group * ahead + 2 * pair
            shift.append(
                jnp.where(on_left, vector[:, first : first + 1], vector[:, first + 1 : first + 2])
            )
        shift = jnp.concatenate(shift, axis=1)
        inverse = inverse_bounds[group]
        whole = jnp.sqrt((members - 1.0) * inverse) * roots[group] + shift * inverse
        for pair in range(ahead // 2):
            combined[group * (ahead // 2) + pair] = whole[:, pair * 128 : pair * 128 + 128]

    for strip in range(batch):
        both = combined[strip // 2]
        other = pltpu.roll(both, members, 1)
        on_diag, off_diag = (both, other) if strip % 2 == 0 else (other, both)
        matrix = jnp.concatenate(
            [jnp.where(on_left, on_diag, 0.0), jnp.where(on_left, 0.0, off_diag)], axis=0
        )
        hi, lo = split(matrix)
        upper, lower = split(turned[strip])
        turned[strip] = dot_nn(
            jnp.concatenate([upper, lower], axis=1), jnp.concatenate([hi, hi], axis=0)
        ) + dot_nn(upper, lo)

    copies = []
    for half in range(halves):
        kind, column = divmod(2 * half, columns)
        result = jnp.transpose(
            jnp.concatenate(
                [turned[strip, half * 8 : half * 8 + 8, :] for strip in range(patches_y)], axis=0
            )
        )
        for step in range(2):
            block = fields_ref[kind, column + step]
            mean = jnp.sum(block, axis=0, keepdims=True) / members
            result_ref[kind, column + step] = (
                mean + result[step * members : step * members + members]
            )
            copies.append(
                pltpu.make_async_copy(
                    result_ref.at[kind, column + step],
                    out_ref.at[:, kind, column + step, :],
                    done_sem.at[kind * columns + column + step],
                )
            )
            copies[-1].start()
    for copy in copies:
        copy.wait()


def analyse(fields, table, extras, entries, counts, width_x, width_y):
    kinds, columns, members, lanes = fields.shape
    tiles, _, slots = extras.shape
    batch = entries.shape[0]
    geometry = (
        width_x, width_y, width_x // TILE_WIDTH_CELLS, width_y // TILE_WIDTH_CELLS,
        lax.axis_size("gy"),
    )
    vmem = pl.BlockSpec(memory_space=pltpu.VMEM)
    return pl.pallas_call(
        functools.partial(analysis_kernel, geometry),
        out_shape=jax.ShapeDtypeStruct((members, kinds, columns, lanes), jnp.float32),
        in_specs=[vmem] * 5,
        out_specs=pl.BlockSpec(memory_space=pl.ANY),
        scratch_shapes=[
            pltpu.VMEM((tiles, batch, slots), jnp.float32),
            pltpu.VMEM((batch, 2 * members, 2 * members), jnp.float32),
            pltpu.VMEM((2 * members, 128), jnp.float32),
            pltpu.VMEM((batch, kinds * columns // 2 * 8, 128), jnp.float32),
            pltpu.VMEM((batch // 2, members, 128), jnp.float32),
            pltpu.VMEM(fields.shape, jnp.float32),
            pltpu.SemaphoreType.DMA((kinds * columns,)),
        ],
        compiler_params=pltpu.CompilerParams(vmem_limit_bytes=40 << 20),
    )(fields, table, extras, entries, counts)


def local(prior_members, obs_column, obs_value, obs_precision, obs_list, patch_count):
    members = prior_members.shape[0]
    levels = prior_members.shape[2]
    width_x = prior_members.shape[3]
    width_y = prior_members.shape[4]
    states = prior_members
    padded = padded_2(states, (("gx", 3), ("gy", 4)), STEPS)
    for repeat in range(STEPS):
        padded = friedrichs_step(cut_outside(padded, STEPS - repeat))
    states = padded
    layer_mean_value = jnp.mean(states[:, 0], axis=1).reshape(members, width_x * width_y)
    columns = obs_column[0, 0]
    members_obs = jnp.take(layer_mean_value, columns, axis=1)
    local_x = (columns // width_y).astype(jnp.float32)
    local_y = (columns % width_y).astype(jnp.float32)
    extras = jnp.stack([obs_value[0, 0], obs_precision[0, 0], local_x, local_y], axis=0)
    obs_info = jnp.concatenate([members_obs, extras], axis=0)[None, None]
    beside_all = padded_2(obs_info, (("gx", 0), ("gy", 1)), 1)
    info_rows, slot_total = beside_all.shape[2:]
    everything = beside_all.reshape(9, info_rows, slot_total)
    fields = jnp.transpose(states, (1, 2, 3, 0, 4)).reshape(
        3 * levels, width_x, members, width_y
    )
    batch = obs_list.shape[0] * obs_list.shape[1]
    result = analyse(
        fields,
        everything[:, :members],
        everything[:, members:],
        obs_list.reshape(batch, obs_list.shape[2]),
        patch_count.reshape(batch, 1),
        width_x,
        width_y,
    )
    return result.reshape(members, 3, levels, width_x, width_y)


def solution(mesh):
    return jax.shard_map(
        local,
        mesh=mesh,
        in_specs=(
            P(None, None, None, "gx", "gy"),
            P("gx", "gy", None),
            P("gx", "gy", None),
            P("gx", "gy", None),
            P("gx", "gy", None),
            P("gx", "gy"),
        ),
        out_specs=P(None, None, None, "gx", "gy"),
        check_vma=False,
    )
```

```python
import functools

import jax
import jax.numpy as jnp
from jax import lax
from jax.experimental import pallas as pl
from jax.experimental.pallas import tpu as pltpu
from jax.sharding import PartitionSpec as P

TILE_WIDTH_CELLS = 8
STEPS = 3
NS_ITERS = 3


courant = 0.3


def split(x):
    hi = x.astype(jnp.bfloat16)
    return hi, (x - hi.astype(jnp.float32)).astype(jnp.bfloat16)


def dot_nn(a, b):
    return lax.dot_general(a, b, (((1,), (0,)), ((), ())), preferred_element_type=jnp.float32)


def dot_nt(a, b):
    return lax.dot_general(a, b, (((1,), (1,)), ((), ())), preferred_element_type=jnp.float32)


NEIGHBOURS = [(x, y) for x in (-1, 0, 1) for y in (-1, 0, 1) if (x, y) != (0, 0)]
CHUNKS = 4


def fluxes(q):
    depth, east, north = q
    height = 1.0 + depth
    inverse = 1.0 / height
    pressure = 0.5 * height * height
    speed = east * inverse
    cross = speed * north
    flux_x = (east, east * speed + pressure, cross)
    flux_y = (north, cross, north * north * inverse + pressure)
    quarter = [0.25 * v for v in q]
    flux_x = [0.5 * courant * f for f in flux_x]
    flux_y = [0.5 * courant * f for f in flux_y]
    return (
        [v - f for v, f in zip(quarter, flux_x)],
        [v + f for v, f in zip(quarter, flux_x)],
        [v - f for v, f in zip(quarter, flux_y)],
        [v + f for v, f in zip(quarter, flux_y)],
    )


def forecast_kernel(
    rows_in_x, rows_in_y, prior_ref, column_ref, value_ref, precision_ref,
    state_ref, table_out, extras_out,
    main, strips, north_strips, south_strips, inserts, table, extras,
    load_sem, halo_send, halo_recv, strip_send, strip_recv, obs_send, obs_recv,
    extra_send, extra_recv,
):
    members, kinds, columns, lanes = prior_ref.shape
    levels = kinds // 3
    slots = column_ref.shape[1]
    pad = STEPS
    wide = columns + 2 * pad
    me_x, me_y = lax.axis_index("gx"), lax.axis_index("gy")

    def there(dx, dy):
        return {"gx": lax.rem(me_x + dx + rows_in_x, rows_in_x), "gy": me_y + dy}

    def exists(dy):
        return (me_y + dy >= 0) & (me_y + dy < rows_in_y)

    def each(act):
        for dx, dy in NEIGHBOURS:
            if dy == 0:
                act(dx, dy)
            else:
                pl.when(exists(dy))(functools.partial(act, dx, dy))

    loads = []
    for column in [*range(columns - pad, columns), *range(columns - pad)]:
        for kind in range(kinds):
            loads.append(
                pltpu.make_async_copy(
                    prior_ref.at[:, kind, column, :], main.at[kind, pad + column],
                    load_sem.at[kind, column],
                )
            )
            loads[-1].start()

    barrier = pltpu.get_barrier_semaphore()

    def greet(dx, dy):
        pl.semaphore_signal(barrier, 1, device_id=there(dx, dy))

    each(greet)
    sides = exists(-1).astype(jnp.int32) + exists(1).astype(jnp.int32)
    pl.semaphore_wait(barrier, 2 + 3 * sides)

    for load in loads:
        load.wait()

    def span(chunk):
        size = members // CHUNKS
        return pl.ds(chunk * size, size)

    def halo(side, chunk):
        start, stop = (columns, 0) if side == 0 else (pad, pad + columns)
        return pltpu.make_async_remote_copy(
            main.at[:, pl.ds(start, pad), span(chunk), :],
            main.at[:, pl.ds(stop, pad), span(chunk), :],
            halo_send.at[side, chunk], halo_recv.at[side, chunk],
            device_id=there(1 - 2 * side, 0),
        )

    def mirrored(dx, dy):
        return (1 - dx) * 3 + 1 - dy

    def seen(dx, dy):
        return (1 + dx) * 3 + 1 + dy

    def strip_copy(dx, dy, source):
        start = {1: columns, 0: pad, -1: pad}[dx]
        stop = {1: 0, 0: pad, -1: pad + columns}[dx]
        count = columns if dx == 0 else pad
        target = {1: south_strips, 0: strips, -1: north_strips}[dy]
        return pltpu.make_async_remote_copy(
            strips.at[:, pl.ds(start, count)], target.at[:, pl.ds(stop, count)],
            strip_send.at[seen(dx, dy)], strip_recv.at[mirrored(dx, dy)],
            device_id=source,
        )

    def table_copy(ref, send, recv, dx, dy, device):
        return pltpu.make_async_remote_copy(
            ref.at[4], ref.at[mirrored(dx, dy)],
            send.at[seen(dx, dy)], recv.at[mirrored(dx, dy)], device_id=device,
        )

    for side in range(2):
        halo(side, 0).start()

    lane = lax.broadcasted_iota(jnp.int32, (8, lanes), 1)
    groups = members // 8
    width = lanes // groups
    half = width // 4
    group_lane = lane % width

    def pack(index, carry):
        kind, column = index // columns, index % columns
        row = main[kind, pad + column]
        packed = jnp.zeros((8, lanes), jnp.float32)
        for group in range(groups):
            part = row[8 * group : 8 * group + 8]
            base = group * width
            upper = pltpu.roll(part, (base + half) % lanes, 1)
            lower = pltpu.roll(part, (base + 3 * half) % lanes, 1)
            packed = jnp.where((lane >= base) & (lane < base + half), upper, packed)
            packed = jnp.where((lane >= base + 3 * half) & (lane < base + width), lower, packed)
        strips[kind, pad + column] = packed
        return carry

    lax.fori_loop(0, kinds * columns, pack, 0)
    each(lambda dx, dy: strip_copy(dx, dy, there(dx, dy)).start())

    where = column_ref[...]
    extras[4, 0:1, :] = value_ref[...]
    extras[4, 1:2, :] = precision_ref[...]
    extras[4, 2:3, :] = lax.div(where, lanes).astype(jnp.float32)
    extras[4, 3:4, :] = lax.rem(where, lanes).astype(jnp.float32)
    extras[4, 4:8, :] = jnp.zeros((4, slots), jnp.float32)
    each(lambda dx, dy: table_copy(extras, extra_send, extra_recv, dx, dy, there(dx, dy)).start())
    for chunk in range(1, CHUNKS):
        for side in range(2):
            halo(side, chunk).start()

    each(lambda dx, dy: strip_copy(-dx, -dy, there(dx, dy)).wait_recv())

    has_north = jnp.where(exists(1), 1.0, 0.0)
    has_south = jnp.where(exists(-1), 1.0, 0.0)
    own = (group_lane < half) | (group_lane >= 3 * half)
    northern = group_lane < 2 * half

    def inside(v):
        kept = jnp.where(northern, has_north, has_south) > 0.5
        return jnp.where((own | kept)[None], v, 0.0)

    for level in range(levels):
        q = []
        for field in range(3):
            kind = field * levels + level
            beyond = jnp.where(
                northern[None],
                pltpu.roll(north_strips[kind], lanes - 2 * half, 2),
                pltpu.roll(south_strips[kind], 2 * half, 2),
            )
            q.append(inside(jnp.where(own[None], strips[kind], beyond)))
        for step in range(STEPS):
            east, west, north, south = fluxes(q)
            rows = q[0].shape[0]
            fresh = []
            for field in range(3):
                up, down = north[field][1 : rows - 1], south[field][1 : rows - 1]
                inserts[step, field * levels + level, 0 : rows - 2] = jnp.where(
                    (group_lane == half)[None], up, pltpu.roll(down, lanes - 2 * half + 2, 2)
                )
                fresh.append(
                    inside(
                        east[field][2:]
                        + west[field][: rows - 2]
                        + pltpu.roll(up, lanes - 1, 2)
                        + pltpu.roll(down, 1, 2)
                    )
                )
            q = fresh

    def advance(index, carry):
        group, level = index // levels, index % levels
        part = pl.ds(pl.multiple_of(group * 8, 8), 8)
        turn = lax.rem(2 * lanes - 1 - half - group * width, lanes)
        q = [main[field * levels + level, :, part, :] for field in range(3)]
        for step in range(STEPS):
            east, west, north, south = fluxes(q)
            rows = q[0].shape[0]
            fresh = []
            for field in range(3):
                edge = pltpu.roll(inserts[step, field * levels + level, 0 : rows - 2], turn, 2)
                up = pltpu.roll(north[field][1 : rows - 1], lanes - 1, 2)
                down = pltpu.roll(south[field][1 : rows - 1], 1, 2)
                fresh.append(
                    east[field][2:]
                    + west[field][: rows - 2]
                    + jnp.where((lane == lanes - 1)[None], edge, up)
                    + jnp.where((lane == 0)[None], edge, down)
                )
            q = fresh
        for field in range(3):
            state_ref[field * levels + level, :, part, :] = q[field]
        return carry

    per_chunk = groups // CHUNKS * levels
    for chunk in range(CHUNKS):
        for side in range(2):
            halo(side, chunk).wait_recv()
        lax.fori_loop(chunk * per_chunk, (chunk + 1) * per_chunk, advance, 0)

    cell = lax.broadcasted_iota(jnp.int32, (lanes, slots), 0)
    observed = jnp.zeros((3 * members, slots), jnp.float32)
    for column in range(columns):
        layers = state_ref[0, column]
        for level in range(1, levels):
            layers = layers + state_ref[level, column]
        layers = layers / levels
        first, rest = split(layers)
        second = layers - first.astype(jnp.float32) - rest.astype(jnp.float32)
        stacked = jnp.concatenate([first, rest, second.astype(jnp.bfloat16)], axis=0)
        chosen = (cell + column * lanes == where).astype(jnp.float32).astype(jnp.bfloat16)
        observed += dot_nn(stacked, chosen)
    table[4] = observed[:members] + observed[members : 2 * members] + observed[2 * members :]
    each(lambda dx, dy: table_copy(table, obs_send, obs_recv, dx, dy, there(dx, dy)).start())

    table_out[4] = table[4]
    extras_out[4] = extras[4]

    def receive(dx, dy):
        for ref, send, recv, out in (
            (extras, extra_send, extra_recv, extras_out),
            (table, obs_send, obs_recv, table_out),
        ):
            table_copy(ref, send, recv, -dx, -dy, there(dx, dy)).wait_recv()
            out[seen(dx, dy)] = ref[seen(dx, dy)]

    each(receive)
    for chunk in range(CHUNKS):
        for side in range(2):
            halo(side, chunk).wait_send()

    def sent(dx, dy):
        strip_copy(dx, dy, there(dx, dy)).wait_send()
        table_copy(extras, extra_send, extra_recv, dx, dy, there(dx, dy)).wait_send()
        table_copy(table, obs_send, obs_recv, dx, dy, there(dx, dy)).wait_send()

    each(sent)


def forecast(prior, obs_column, obs_value, obs_precision):
    members, kinds, columns, lanes = prior.shape
    slots = obs_column.shape[1]
    wide = columns + 2 * STEPS
    vmem = pl.BlockSpec(memory_space=pltpu.VMEM)
    return pl.pallas_call(
        functools.partial(forecast_kernel, lax.axis_size("gx"), lax.axis_size("gy")),
        out_shape=(
            jax.ShapeDtypeStruct((kinds, columns, members, lanes), jnp.float32),
            jax.ShapeDtypeStruct((9, members, slots), jnp.float32),
            jax.ShapeDtypeStruct((9, 8, slots), jnp.float32),
        ),
        in_specs=[pl.BlockSpec(memory_space=pl.ANY), vmem, vmem, vmem],
        out_specs=(vmem, vmem, vmem),
        scratch_shapes=[
            pltpu.VMEM((kinds, wide, members, lanes), jnp.float32),
            pltpu.VMEM((kinds, wide, 8, lanes), jnp.float32),
            pltpu.VMEM((kinds, wide, 8, lanes), jnp.float32),
            pltpu.VMEM((kinds, wide, 8, lanes), jnp.float32),
            pltpu.VMEM((STEPS, kinds, wide, 8, lanes), jnp.float32),
            pltpu.VMEM((9, members, slots), jnp.float32),
            pltpu.VMEM((9, 8, slots), jnp.float32),
            pltpu.SemaphoreType.DMA((kinds, columns)),
            pltpu.SemaphoreType.DMA((2, CHUNKS)),
            pltpu.SemaphoreType.DMA((2, CHUNKS)),
        ]
        + [pltpu.SemaphoreType.DMA((9,))] * 6,
        compiler_params=pltpu.CompilerParams(
            collective_id=0, has_side_effects=True, vmem_limit_bytes=24 << 20
        ),
    )(prior, obs_column, obs_value, obs_precision)


def analysis_kernel(
    geometry, fields_ref, table_ref, extras_ref, list_ref, count_ref, out_ref,
    weights, gram, force, turned, combined, result_ref, done_sem,
):
    width_x, width_y, patches_x, patches_y, rows_in_y = geometry
    kinds, columns, members, lanes = fields_ref.shape
    tiles, _, slots = extras_ref.shape
    batch, capacity = list_ref.shape
    per_tile = slots // 128
    halves = kinds * columns // 2

    chunks = tiles * per_tile
    padded_chunks = -(-chunks // 8) * 8
    usable_at = lax.broadcasted_iota(jnp.int32, (1, capacity), 1)
    chunk_id = lax.broadcasted_iota(jnp.int32, (padded_chunks, capacity), 0)
    lane_id = lax.broadcasted_iota(jnp.int32, (128, capacity), 0)
    for patch in range(batch):
        named = list_ref[patch : patch + 1, :]
        usable = usable_at < count_ref[patch : patch + 1, :]
        upper = jnp.where(usable, named // 128, -1)
        lower = named % 128
        counts = dot_nt(
            (chunk_id == upper).astype(jnp.float32).astype(jnp.bfloat16),
            (lane_id == lower).astype(jnp.float32).astype(jnp.bfloat16),
        )
        for chunk in range(chunks):
            tile, part = divmod(chunk, per_tile)
            weights[tile, patch : patch + 1, part * 128 : part * 128 + 128] = counts[
                chunk : chunk + 1
            ]

    patch_id = lax.broadcasted_iota(jnp.int32, (batch, slots), 0)
    centre_x = (patch_id // patches_y * TILE_WIDTH_CELLS).astype(jnp.float32) + (
        TILE_WIDTH_CELLS - 1
    ) * 0.5
    centre_y = (patch_id % patches_y * TILE_WIDTH_CELLS).astype(jnp.float32) + (
        TILE_WIDTH_CELLS - 1
    ) * 0.5
    gram[...] = jnp.zeros_like(gram)
    force[...] = jnp.zeros_like(force)
    for tile in range(tiles):
        shift_x, shift_y = tile // 3 - 1, tile % 3 - 1

        def add_tile():
            info = extras_ref[tile]
            offset_x = shift_x * width_x + info[2:3] - centre_x
            offset_y = shift_y * width_y + info[3:4] - centre_y
            near = jnp.exp(-((offset_x / width_x) ** 2) - (offset_y / width_y) ** 2)
            factor = weights[tile] * info[1:2] * near
            values = table_ref[tile]
            mean = jnp.sum(values, axis=0, keepdims=True) / members
            pert = values - mean
            upper, lower = split(pert)
            both = jnp.concatenate([upper, lower], axis=0)
            for patch in range(batch):
                first, second = split(pert * factor[patch : patch + 1])
                gram[patch] += dot_nt(jnp.concatenate([first, second], axis=0), both)
            first, second = split(factor * (info[0:1] - mean))
            rest = jnp.zeros((128 - 2 * batch, slots), jnp.bfloat16)
            force[...] += dot_nt(both, jnp.concatenate([first, second, rest], axis=0))

        row = lax.axis_index("gy") + shift_y
        pl.when((row >= 0) & (row < rows_in_y))(add_tile)

    for half in range(halves):
        kind, column = divmod(2 * half, columns)
        pair = []
        for step in range(2):
            block = fields_ref[kind, column + step]
            pair.append(block - jnp.sum(block, axis=0, keepdims=True) / members)
        flipped = jnp.transpose(jnp.concatenate(pair, axis=0))
        for strip in range(patches_y):
            turned[strip, half * 8 : half * 8 + 8, :] = flipped[strip * 8 : strip * 8 + 8]

    ahead = 256 // members
    groups = batch // ahead
    lane128 = lax.broadcasted_iota(jnp.int32, (members, 128), 1)
    own_row = lax.broadcasted_iota(jnp.int32, (members, 128), 0)
    diagonal = lane128 % members == own_row
    on_left = lane128 < members
    identity1 = jnp.where(diagonal, 1.0, 0.0)
    identity = jnp.concatenate([identity1, identity1], axis=1)
    in_block = (
        lax.broadcasted_iota(jnp.int32, (256, 256), 0) // members
        == lax.broadcasted_iota(jnp.int32, (256, 256), 1) // members
    ).astype(jnp.float32).astype(jnp.bfloat16)

    def tiled(part):
        return jnp.concatenate([part] * ahead, axis=0) * in_block

    def left(x):
        hi, lo = split(x)
        return jnp.concatenate([hi, lo], axis=0), hi

    def right(x):
        hi, lo = split(x)
        return tiled(hi), tiled(lo)

    def product(x, y):
        both = dot_nn(x[0], y[0])
        return both[:members] + both[members:] + dot_nn(x[1], y[1])

    scaled, inverse_bounds = [], []
    for group in range(groups):
        parts, bounds = [], []
        for pair in range(ahead // 2):
            even = gram[group * ahead + 2 * pair]
            odd = gram[group * ahead + 2 * pair + 1]
            matrix = jnp.where(
                on_left,
                even[:members] + pltpu.roll(even[:members], members, 1) + even[members:],
                odd[:members]
                + pltpu.roll(odd[:members], members, 1)
                + pltpu.roll(odd[members:], members, 1),
            )
            trace = jnp.where(diagonal, matrix, 0.0)
            first = jnp.sum(jnp.where(on_left, trace, 0.0), keepdims=True)
            second = jnp.sum(jnp.where(on_left, 0.0, trace), keepdims=True)
            bounds.append(members - 1.0 + jnp.where(on_left[:1], first, second))
            parts.append(matrix)
        bounds = jnp.concatenate(bounds, axis=1)
        matrix = jnp.concatenate(parts, axis=1)
        scaled.append((matrix + (members - 1.0) * identity) / bounds)
        inverse_bounds.append(1.0 / bounds)

    iterate = [left(a) for a in scaled]
    values = scaled
    factors = [1.5 * identity - 0.5 * a for a in scaled]
    roots = factors
    for repeat in range(1, NS_ITERS):
        factor_right = [right(s) for s in factors]
        iterate = [left(v) for v in values]
        values = [product(y, s) for y, s in zip(iterate, factor_right)]
        root_left = [left(z) for z in roots]
        value_right = [right(v) for v in values]
        factors = [
            1.5 * identity - 0.5 * product(z, y) for z, y in zip(root_left, value_right)
        ]
        factor_left = [left(s) for s in factors]
        root_right = [right(z) for z in roots]
        roots = [product(s, z) for s, z in zip(factor_left, root_right)]

    total = force[...]
    forcing = (
        total[:members] + pltpu.roll(total[:members], 128 - batch, 1) + total[members:]
    )
    block_row = lax.broadcasted_iota(jnp.int32, (256, 128), 0) // members
    block_lane = lax.broadcasted_iota(jnp.int32, (256, 128), 1)
    for group in range(groups):
        root = left(roots[group])
        keep = (block_row + group * ahead == block_lane).astype(jnp.float32).astype(jnp.bfloat16)
        vector = forcing
        for repeat in range(2):
            hi, lo = split(vector)
            hi = jnp.concatenate([hi] * ahead, axis=0) * keep
            lo = jnp.concatenate([lo] * ahead, axis=0) * keep
            vector = product(root, (hi, lo))
        shift = []
        for pair in range(ahead // 2):
            first = group * ahead + 2 * pair
            shift.append(
                jnp.where(on_left, vector[:, first : first + 1], vector[:, first + 1 : first + 2])
            )
        shift = jnp.concatenate(shift, axis=1)
        inverse = inverse_bounds[group]
        whole = jnp.sqrt((members - 1.0) * inverse) * roots[group] + shift * inverse
        for pair in range(ahead // 2):
            combined[group * (ahead // 2) + pair] = whole[:, pair * 128 : pair * 128 + 128]

    for strip in range(batch):
        both = combined[strip // 2]
        other = pltpu.roll(both, members, 1)
        on_diag, off_diag = (both, other) if strip % 2 == 0 else (other, both)
        matrix = jnp.concatenate(
            [jnp.where(on_left, on_diag, 0.0), jnp.where(on_left, 0.0, off_diag)], axis=0
        )
        hi, lo = split(matrix)
        upper, lower = split(turned[strip])
        turned[strip] = dot_nn(
            jnp.concatenate([upper, lower], axis=1), jnp.concatenate([hi, hi], axis=0)
        ) + dot_nn(upper, lo)

    copies = []
    for half in range(halves):
        kind, column = divmod(2 * half, columns)
        result = jnp.transpose(
            jnp.concatenate(
                [turned[strip, half * 8 : half * 8 + 8, :] for strip in range(patches_y)], axis=0
            )
        )
        for step in range(2):
            block = fields_ref[kind, column + step]
            mean = jnp.sum(block, axis=0, keepdims=True) / members
            result_ref[kind, column + step] = (
                mean + result[step * members : step * members + members]
            )
            copies.append(
                pltpu.make_async_copy(
                    result_ref.at[kind, column + step],
                    out_ref.at[:, kind, column + step, :],
                    done_sem.at[kind * columns + column + step],
                )
            )
            copies[-1].start()
    for copy in copies:
        copy.wait()


def analyse(fields, table, extras, entries, counts, width_x, width_y):
    kinds, columns, members, lanes = fields.shape
    tiles, _, slots = extras.shape
    batch = entries.shape[0]
    geometry = (
        width_x, width_y, width_x // TILE_WIDTH_CELLS, width_y // TILE_WIDTH_CELLS,
        lax.axis_size("gy"),
    )
    vmem = pl.BlockSpec(memory_space=pltpu.VMEM)
    return pl.pallas_call(
        functools.partial(analysis_kernel, geometry),
        out_shape=jax.ShapeDtypeStruct((members, kinds, columns, lanes), jnp.float32),
        in_specs=[vmem] * 5,
        out_specs=pl.BlockSpec(memory_space=pl.ANY),
        scratch_shapes=[
            pltpu.VMEM((tiles, batch, slots), jnp.float32),
            pltpu.VMEM((batch, 2 * members, 2 * members), jnp.float32),
            pltpu.VMEM((2 * members, 128), jnp.float32),
            pltpu.VMEM((batch, kinds * columns // 2 * 8, 128), jnp.float32),
            pltpu.VMEM((batch // 2, members, 128), jnp.float32),
            pltpu.VMEM(fields.shape, jnp.float32),
            pltpu.SemaphoreType.DMA((kinds * columns,)),
        ],
        compiler_params=pltpu.CompilerParams(vmem_limit_bytes=24 << 20),
    )(fields, table, extras, entries, counts)


def local(prior_members, obs_column, obs_value, obs_precision, obs_list, patch_count):
    members, fields, levels, width_x, width_y = prior_members.shape
    state, table, extras = forecast(
        prior_members.reshape(members, fields * levels, width_x, width_y),
        obs_column[0], obs_value[0], obs_precision[0],
    )
    batch = obs_list.shape[0] * obs_list.shape[1]
    result = analyse(
        state,
        table,
        extras,
        obs_list.reshape(batch, obs_list.shape[2]),
        patch_count.reshape(batch, 1),
        width_x,
        width_y,
    )
    return result.reshape(prior_members.shape)


def solution(mesh):
    return jax.shard_map(
        local,
        mesh=mesh,
        in_specs=(
            P(None, None, None, "gx", "gy"),
            P("gx", "gy", None),
            P("gx", "gy", None),
            P("gx", "gy", None),
            P("gx", "gy", None),
            P("gx", "gy"),
        ),
        out_specs=P(None, None, None, "gx", "gy"),
        check_vma=False,
    )
```

```python
import functools

import jax
import jax.numpy as jnp
from jax import lax
from jax.experimental import pallas as pl
from jax.experimental.pallas import tpu as pltpu
from jax.sharding import PartitionSpec as P

TILE_WIDTH_CELLS = 8
STEPS = 3
NS_ITERS = 3


courant = 0.3


def split(x):
    hi = x.astype(jnp.bfloat16)
    return hi, (x - hi.astype(jnp.float32)).astype(jnp.bfloat16)


def dot_nn(a, b):
    return lax.dot_general(a, b, (((1,), (0,)), ((), ())), preferred_element_type=jnp.float32)


def dot_nt(a, b):
    return lax.dot_general(a, b, (((1,), (1,)), ((), ())), preferred_element_type=jnp.float32)


NEIGHBOURS = [(x, y) for x in (-1, 0, 1) for y in (-1, 0, 1) if (x, y) != (0, 0)]
CHUNKS = 4


def fluxes(q):
    depth, east, north = q
    height = 1.0 + depth
    inverse = 1.0 / height
    pressure = 0.5 * height * height
    speed = east * inverse
    cross = speed * north
    flux_x = (east, east * speed + pressure, cross)
    flux_y = (north, cross, north * north * inverse + pressure)
    quarter = [0.25 * v for v in q]
    flux_x = [0.5 * courant * f for f in flux_x]
    flux_y = [0.5 * courant * f for f in flux_y]
    return (
        [v - f for v, f in zip(quarter, flux_x)],
        [v + f for v, f in zip(quarter, flux_x)],
        [v - f for v, f in zip(quarter, flux_y)],
        [v + f for v, f in zip(quarter, flux_y)],
    )


def forecast_kernel(
    rows_in_x, rows_in_y, prior_ref, column_ref, value_ref, precision_ref,
    state_ref, table_out, extras_out,
    main, strips, dense_north, dense_south, north_strips, south_strips, inserts, table,
    extras, column_vmem, info_sem, load_sem, halo_send, halo_recv, strip_send, strip_recv, obs_send, obs_recv,
    extra_send, extra_recv,
):
    members, kinds, columns, lanes = prior_ref.shape
    levels = kinds // 3
    slots = column_ref.shape[1]
    pad = STEPS
    wide = columns + 2 * pad
    me_x, me_y = lax.axis_index("gx"), lax.axis_index("gy")

    def there(dx, dy):
        return {"gx": lax.rem(me_x + dx + rows_in_x, rows_in_x), "gy": me_y + dy}

    def exists(dy):
        return (me_y + dy >= 0) & (me_y + dy < rows_in_y)

    def each(act):
        for dx, dy in NEIGHBOURS:
            if dy == 0:
                act(dx, dy)
            else:
                pl.when(exists(dy))(functools.partial(act, dx, dy))

    loads = []
    for column in [*range(columns - pad, columns), *range(columns - pad)]:
        for kind in range(kinds):
            loads.append(
                pltpu.make_async_copy(
                    prior_ref.at[:, kind, column, :], main.at[kind, pad + column],
                    load_sem.at[kind, column],
                )
            )
            loads[-1].start()
    for index, (source, target) in enumerate(
        (
            (column_ref, column_vmem),
            (value_ref, extras.at[4, 0:1]),
            (precision_ref, extras.at[4, 1:2]),
        )
    ):
        loads.append(pltpu.make_async_copy(source, target, info_sem.at[index]))
        loads[-1].start()

    barrier = pltpu.get_barrier_semaphore()

    def greet(dx, dy):
        pl.semaphore_signal(barrier, 1, device_id=there(dx, dy))

    each(greet)
    sides = exists(-1).astype(jnp.int32) + exists(1).astype(jnp.int32)
    pl.semaphore_wait(barrier, 2 + 3 * sides)

    for load in loads:
        load.wait()

    def span(chunk):
        size = members // CHUNKS
        return pl.ds(chunk * size, size)

    def halo(side, chunk):
        start, stop = (columns, 0) if side == 0 else (pad, pad + columns)
        return pltpu.make_async_remote_copy(
            main.at[:, pl.ds(start, pad), span(chunk), :],
            main.at[:, pl.ds(stop, pad), span(chunk), :],
            halo_send.at[side, chunk], halo_recv.at[side, chunk],
            device_id=there(1 - 2 * side, 0),
        )

    def mirrored(dx, dy):
        return (1 - dx) * 3 + 1 - dy

    def seen(dx, dy):
        return (1 + dx) * 3 + 1 + dy

    def strip_copy(dx, dy, device):
        start = {1: columns, 0: pad, -1: pad}[dx]
        stop = {1: 0, 0: pad, -1: pad + columns}[dx]
        count = columns if dx == 0 else pad
        target = {1: south_strips, 0: strips, -1: north_strips}[dy]
        source = {1: dense_north, 0: strips, -1: dense_south}[dy]
        start = start if dy == 0 else start - pad
        return pltpu.make_async_remote_copy(
            source.at[:, pl.ds(start, count)], target.at[:, pl.ds(stop, count)],
            strip_send.at[seen(dx, dy)], strip_recv.at[mirrored(dx, dy)],
            device_id=device,
        )

    def table_copy(ref, send, recv, dx, dy, device):
        return pltpu.make_async_remote_copy(
            ref.at[4], ref.at[mirrored(dx, dy)],
            send.at[seen(dx, dy)], recv.at[mirrored(dx, dy)], device_id=device,
        )

    for side in range(2):
        halo(side, 0).start()

    lane = lax.broadcasted_iota(jnp.int32, (8, lanes), 1)
    groups = members // 8
    width = lanes // groups
    half = width // 4
    group_lane = lane % width

    def pack(kind, carry):
        raw = jnp.zeros((columns, 8, lanes), jnp.float32)
        for group in range(groups):
            part = main[kind, pad : pad + columns, 8 * group : 8 * group + 8, :]
            base = group * width
            moved = pltpu.roll(part, base + half, 2)
            raw = jnp.where(((lane >= base) & (lane < base + width))[None], moved, raw)
        strips[kind, pad : pad + columns] = jnp.where(
            (group_lane < half)[None], raw, pltpu.roll(raw, 2 * half, 2)
        )
        return carry

    lax.fori_loop(0, kinds, pack, 0)
    for level in range(levels):
        for dense, place in ((dense_north, 0), (dense_south, 3)):
            tile = None
            for field in range(3):
                piece = strips[field * levels + level, pad : pad + columns]
                shift = (field - place) * half % lanes
                piece = pltpu.roll(piece, shift, 2) if shift else piece
                tile = piece if field == 0 else jnp.where(
                    (group_lane // half == field)[None], piece, tile
                )
            dense[level] = tile
    each(lambda dx, dy: strip_copy(dx, dy, there(dx, dy)).start())

    where = column_vmem[...]
    extras[4, 2:3, :] = lax.div(where, lanes).astype(jnp.float32)
    extras[4, 3:4, :] = lax.rem(where, lanes).astype(jnp.float32)
    extras[4, 4:8, :] = jnp.zeros((4, slots), jnp.float32)
    each(lambda dx, dy: table_copy(extras, extra_send, extra_recv, dx, dy, there(dx, dy)).start())
    for chunk in range(1, CHUNKS):
        for side in range(2):
            halo(side, chunk).start()

    each(lambda dx, dy: strip_copy(-dx, -dy, there(dx, dy)).wait_recv())

    has_north = jnp.where(exists(1), 1.0, 0.0)
    has_south = jnp.where(exists(-1), 1.0, 0.0)
    own = (group_lane < half) | (group_lane >= 3 * half)
    northern = group_lane < 2 * half

    def inside(v):
        kept = jnp.where(northern, has_north, has_south) > 0.5
        return jnp.where((own | kept)[None], v, 0.0)

    for level in range(levels):
        q = []
        for field in range(3):
            kind = field * levels + level
            beyond = jnp.where(
                northern[None],
                pltpu.roll(north_strips[level], (1 - field) * half % lanes, 2),
                pltpu.roll(south_strips[level], (2 - field) * half % lanes, 2),
            )
            q.append(inside(jnp.where(own[None], strips[kind], beyond)))
        for step in range(STEPS):
            east, west, north, south = fluxes(q)
            rows = q[0].shape[0]
            fresh = []
            for field in range(3):
                up, down = north[field][1 : rows - 1], south[field][1 : rows - 1]
                inserts[step, field * levels + level, 0 : rows - 2] = jnp.where(
                    (group_lane == half)[None], up, pltpu.roll(down, lanes - 2 * half + 2, 2)
                )
                fresh.append(
                    inside(
                        east[field][2:]
                        + west[field][: rows - 2]
                        + pltpu.roll(up, lanes - 1, 2)
                        + pltpu.roll(down, 1, 2)
                    )
                )
            q = fresh

    def advance(index, carry):
        group, level = index // levels, index % levels
        part = pl.ds(pl.multiple_of(group * 8, 8), 8)
        turn = lax.rem(2 * lanes - 1 - half - group * width, lanes)
        q = [main[field * levels + level, :, part, :] for field in range(3)]
        for step in range(STEPS):
            east, west, north, south = fluxes(q)
            rows = q[0].shape[0]
            fresh = []
            for field in range(3):
                edge = pltpu.roll(inserts[step, field * levels + level, 0 : rows - 2], turn, 2)
                up = pltpu.roll(north[field][1 : rows - 1], lanes - 1, 2)
                down = pltpu.roll(south[field][1 : rows - 1], 1, 2)
                fresh.append(
                    east[field][2:]
                    + west[field][: rows - 2]
                    + jnp.where((lane == lanes - 1)[None], edge, up)
                    + jnp.where((lane == 0)[None], edge, down)
                )
            q = fresh
        for field in range(3):
            state_ref[field * levels + level, :, part, :] = q[field]
        return carry

    per_chunk = groups // CHUNKS * levels
    for chunk in range(CHUNKS):
        for side in range(2):
            halo(side, chunk).wait_recv()
        lax.fori_loop(chunk * per_chunk, (chunk + 1) * per_chunk, advance, 0)

    cell = lax.broadcasted_iota(jnp.int32, (lanes, slots), 0)
    observed = jnp.zeros((3 * members, slots), jnp.float32)
    for column in range(columns):
        layers = state_ref[0, column]
        for level in range(1, levels):
            layers = layers + state_ref[level, column]
        layers = layers / levels
        first, rest = split(layers)
        second = layers - first.astype(jnp.float32) - rest.astype(jnp.float32)
        stacked = jnp.concatenate([first, rest, second.astype(jnp.bfloat16)], axis=0)
        chosen = (cell + column * lanes == where).astype(jnp.float32).astype(jnp.bfloat16)
        observed += dot_nn(stacked, chosen)
    table[4] = observed[:members] + observed[members : 2 * members] + observed[2 * members :]
    each(lambda dx, dy: table_copy(table, obs_send, obs_recv, dx, dy, there(dx, dy)).start())

    table_out[4] = table[4]
    extras_out[4] = extras[4]

    def receive(dx, dy):
        for ref, send, recv, out in (
            (extras, extra_send, extra_recv, extras_out),
            (table, obs_send, obs_recv, table_out),
        ):
            table_copy(ref, send, recv, -dx, -dy, there(dx, dy)).wait_recv()
            out[seen(dx, dy)] = ref[seen(dx, dy)]

    each(receive)
    for chunk in range(CHUNKS):
        for side in range(2):
            halo(side, chunk).wait_send()

    def sent(dx, dy):
        strip_copy(dx, dy, there(dx, dy)).wait_send()
        table_copy(extras, extra_send, extra_recv, dx, dy, there(dx, dy)).wait_send()
        table_copy(table, obs_send, obs_recv, dx, dy, there(dx, dy)).wait_send()

    each(sent)


def forecast(prior, obs_column, obs_value, obs_precision):
    members, kinds, columns, lanes = prior.shape
    slots = obs_column.shape[1]
    wide = columns + 2 * STEPS
    vmem = pl.BlockSpec(memory_space=pltpu.VMEM)
    return pl.pallas_call(
        functools.partial(forecast_kernel, lax.axis_size("gx"), lax.axis_size("gy")),
        out_shape=(
            jax.ShapeDtypeStruct((kinds, columns, members, lanes), jnp.float32),
            jax.ShapeDtypeStruct((9, members, slots), jnp.float32),
            jax.ShapeDtypeStruct((9, 8, slots), jnp.float32),
        ),
        in_specs=[pl.BlockSpec(memory_space=pltpu.HBM)] * 4,
        out_specs=(vmem, vmem, vmem),
        scratch_shapes=[
            pltpu.VMEM((kinds, wide, members, lanes), jnp.float32),
            pltpu.VMEM((kinds, wide, 8, lanes), jnp.float32),
            pltpu.VMEM((kinds // 3, columns, 8, lanes), jnp.float32),
            pltpu.VMEM((kinds // 3, columns, 8, lanes), jnp.float32),
            pltpu.VMEM((kinds // 3, wide, 8, lanes), jnp.float32),
            pltpu.VMEM((kinds // 3, wide, 8, lanes), jnp.float32),
            pltpu.VMEM((STEPS, kinds, wide, 8, lanes), jnp.float32),
            pltpu.VMEM((9, members, slots), jnp.float32),
            pltpu.VMEM((9, 8, slots), jnp.float32),
            pltpu.VMEM((1, slots), jnp.int32),
            pltpu.SemaphoreType.DMA((3,)),
            pltpu.SemaphoreType.DMA((kinds, columns)),
            pltpu.SemaphoreType.DMA((2, CHUNKS)),
            pltpu.SemaphoreType.DMA((2, CHUNKS)),
        ]
        + [pltpu.SemaphoreType.DMA((9,))] * 6,
        compiler_params=pltpu.CompilerParams(
            collective_id=0, has_side_effects=True, vmem_limit_bytes=24 << 20
        ),
    )(prior, obs_column, obs_value, obs_precision)


def analysis_kernel(
    geometry, fields_ref, table_ref, extras_ref, list_ref, count_ref, out_ref,
    weights, gram, force, turned, combined, result_ref, done_sem,
):
    width_x, width_y, patches_x, patches_y, rows_in_y = geometry
    kinds, columns, members, lanes = fields_ref.shape
    tiles, _, slots = extras_ref.shape
    batch, capacity = list_ref.shape
    per_tile = slots // 128
    halves = kinds * columns // 2

    chunks = tiles * per_tile
    padded_chunks = -(-chunks // 8) * 8
    usable_at = lax.broadcasted_iota(jnp.int32, (1, capacity), 1)
    chunk_id = lax.broadcasted_iota(jnp.int32, (padded_chunks, capacity), 0)
    lane_id = lax.broadcasted_iota(jnp.int32, (128, capacity), 0)
    for patch in range(batch):
        named = list_ref[patch : patch + 1, :]
        usable = usable_at < count_ref[patch // patches_y, patch % patches_y]
        upper = jnp.where(usable, named // 128, -1)
        lower = named % 128
        counts = dot_nt(
            (chunk_id == upper).astype(jnp.float32).astype(jnp.bfloat16),
            (lane_id == lower).astype(jnp.float32).astype(jnp.bfloat16),
        )
        for chunk in range(chunks):
            tile, part = divmod(chunk, per_tile)
            weights[tile, patch : patch + 1, part * 128 : part * 128 + 128] = counts[
                chunk : chunk + 1
            ]

    patch_id = lax.broadcasted_iota(jnp.int32, (batch, slots), 0)
    centre_x = (patch_id // patches_y * TILE_WIDTH_CELLS).astype(jnp.float32) + (
        TILE_WIDTH_CELLS - 1
    ) * 0.5
    centre_y = (patch_id % patches_y * TILE_WIDTH_CELLS).astype(jnp.float32) + (
        TILE_WIDTH_CELLS - 1
    ) * 0.5
    gram[...] = jnp.zeros_like(gram)
    force[...] = jnp.zeros_like(force)
    for tile in range(tiles):
        shift_x, shift_y = tile // 3 - 1, tile % 3 - 1

        def add_tile():
            info = extras_ref[tile]
            offset_x = shift_x * width_x + info[2:3] - centre_x
            offset_y = shift_y * width_y + info[3:4] - centre_y
            near = jnp.exp(-((offset_x / width_x) ** 2) - (offset_y / width_y) ** 2)
            factor = weights[tile] * info[1:2] * near
            values = table_ref[tile]
            mean = jnp.sum(values, axis=0, keepdims=True) / members
            pert = values - mean
            upper, lower = split(pert)
            both = jnp.concatenate([upper, lower], axis=0)
            for patch in range(batch):
                first, second = split(pert * factor[patch : patch + 1])
                gram[patch] += dot_nt(jnp.concatenate([first, second], axis=0), both)
            first, second = split(factor * (info[0:1] - mean))
            rest = jnp.zeros((128 - 2 * batch, slots), jnp.bfloat16)
            force[...] += dot_nt(both, jnp.concatenate([first, second, rest], axis=0))

        row = lax.axis_index("gy") + shift_y
        pl.when((row >= 0) & (row < rows_in_y))(add_tile)

    for half in range(halves):
        kind, column = divmod(2 * half, columns)
        pair = []
        for step in range(2):
            block = fields_ref[kind, column + step]
            pair.append(block - jnp.sum(block, axis=0, keepdims=True) / members)
        flipped = jnp.transpose(jnp.concatenate(pair, axis=0))
        for strip in range(patches_y):
            turned[strip, half * 8 : half * 8 + 8, :] = flipped[strip * 8 : strip * 8 + 8]

    ahead = 256 // members
    groups = batch // ahead
    lane128 = lax.broadcasted_iota(jnp.int32, (members, 128), 1)
    own_row = lax.broadcasted_iota(jnp.int32, (members, 128), 0)
    diagonal = lane128 % members == own_row
    on_left = lane128 < members
    identity1 = jnp.where(diagonal, 1.0, 0.0)
    identity = jnp.concatenate([identity1, identity1], axis=1)
    in_block = (
        lax.broadcasted_iota(jnp.int32, (256, 256), 0) // members
        == lax.broadcasted_iota(jnp.int32, (256, 256), 1) // members
    ).astype(jnp.float32).astype(jnp.bfloat16)

    def tiled(part):
        return jnp.concatenate([part] * ahead, axis=0) * in_block

    def left(x):
        hi, lo = split(x)
        return jnp.concatenate([hi, lo], axis=0), hi

    def right(x):
        hi, lo = split(x)
        return tiled(hi), tiled(lo)

    def product(x, y):
        both = dot_nn(x[0], y[0])
        return both[:members] + both[members:] + dot_nn(x[1], y[1])

    scaled, inverse_bounds = [], []
    for group in range(groups):
        parts, bounds = [], []
        for pair in range(ahead // 2):
            even = gram[group * ahead + 2 * pair]
            odd = gram[group * ahead + 2 * pair + 1]
            matrix = jnp.where(
                on_left,
                even[:members] + pltpu.roll(even[:members], members, 1) + even[members:],
                odd[:members]
                + pltpu.roll(odd[:members], members, 1)
                + pltpu.roll(odd[members:], members, 1),
            )
            trace = jnp.where(diagonal, matrix, 0.0)
            first = jnp.sum(jnp.where(on_left, trace, 0.0), keepdims=True)
            second = jnp.sum(jnp.where(on_left, 0.0, trace), keepdims=True)
            bounds.append(members - 1.0 + jnp.where(on_left[:1], first, second))
            parts.append(matrix)
        bounds = jnp.concatenate(bounds, axis=1)
        matrix = jnp.concatenate(parts, axis=1)
        scaled.append((matrix + (members - 1.0) * identity) / bounds)
        inverse_bounds.append(1.0 / bounds)

    iterate = [left(a) for a in scaled]
    values = scaled
    factors = [1.5 * identity - 0.5 * a for a in scaled]
    roots = factors
    for repeat in range(1, NS_ITERS):
        factor_right = [right(s) for s in factors]
        iterate = [left(v) for v in values]
        values = [product(y, s) for y, s in zip(iterate, factor_right)]
        root_left = [left(z) for z in roots]
        value_right = [right(v) for v in values]
        factors = [
            1.5 * identity - 0.5 * product(z, y) for z, y in zip(root_left, value_right)
        ]
        factor_left = [left(s) for s in factors]
        root_right = [right(z) for z in roots]
        roots = [product(s, z) for s, z in zip(factor_left, root_right)]

    total = force[...]
    forcing = (
        total[:members] + pltpu.roll(total[:members], 128 - batch, 1) + total[members:]
    )
    block_row = lax.broadcasted_iota(jnp.int32, (256, 128), 0) // members
    block_lane = lax.broadcasted_iota(jnp.int32, (256, 128), 1)
    for group in range(groups):
        root = left(roots[group])
        keep = (block_row + group * ahead == block_lane).astype(jnp.float32).astype(jnp.bfloat16)
        vector = forcing
        for repeat in range(2):
            hi, lo = split(vector)
            hi = jnp.concatenate([hi] * ahead, axis=0) * keep
            lo = jnp.concatenate([lo] * ahead, axis=0) * keep
            vector = product(root, (hi, lo))
        shift = []
        for pair in range(ahead // 2):
            first = group * ahead + 2 * pair
            shift.append(
                jnp.where(on_left, vector[:, first : first + 1], vector[:, first + 1 : first + 2])
            )
        shift = jnp.concatenate(shift, axis=1)
        inverse = inverse_bounds[group]
        whole = jnp.sqrt((members - 1.0) * inverse) * roots[group] + shift * inverse
        for pair in range(ahead // 2):
            combined[group * (ahead // 2) + pair] = whole[:, pair * 128 : pair * 128 + 128]

    for strip in range(batch):
        both = combined[strip // 2]
        other = pltpu.roll(both, members, 1)
        on_diag, off_diag = (both, other) if strip % 2 == 0 else (other, both)
        matrix = jnp.concatenate(
            [jnp.where(on_left, on_diag, 0.0), jnp.where(on_left, 0.0, off_diag)], axis=0
        )
        hi, lo = split(matrix)
        upper, lower = split(turned[strip])
        turned[strip] = dot_nn(
            jnp.concatenate([upper, lower], axis=1), jnp.concatenate([hi, hi], axis=0)
        ) + dot_nn(upper, lo)

    copies = []
    for half in range(halves):
        kind, column = divmod(2 * half, columns)
        result = jnp.transpose(
            jnp.concatenate(
                [turned[strip, half * 8 : half * 8 + 8, :] for strip in range(patches_y)], axis=0
            )
        )
        for step in range(2):
            block = fields_ref[kind, column + step]
            mean = jnp.sum(block, axis=0, keepdims=True) / members
            result_ref[kind, column + step] = (
                mean + result[step * members : step * members + members]
            )
            copies.append(
                pltpu.make_async_copy(
                    result_ref.at[kind, column + step],
                    out_ref.at[:, kind, column + step, :],
                    done_sem.at[kind * columns + column + step],
                )
            )
            copies[-1].start()
    for copy in copies:
        copy.wait()


def analyse(fields, table, extras, entries, counts, width_x, width_y):
    kinds, columns, members, lanes = fields.shape
    tiles, _, slots = extras.shape
    batch = entries.shape[0]
    geometry = (
        width_x, width_y, width_x // TILE_WIDTH_CELLS, width_y // TILE_WIDTH_CELLS,
        lax.axis_size("gy"),
    )
    vmem = pl.BlockSpec(memory_space=pltpu.VMEM)
    return pl.pallas_call(
        functools.partial(analysis_kernel, geometry),
        out_shape=jax.ShapeDtypeStruct((members, kinds, columns, lanes), jnp.float32),
        in_specs=[vmem] * 4 + [pl.BlockSpec(memory_space=pltpu.SMEM)],
        out_specs=pl.BlockSpec(memory_space=pl.ANY),
        scratch_shapes=[
            pltpu.VMEM((tiles, batch, slots), jnp.float32),
            pltpu.VMEM((batch, 2 * members, 2 * members), jnp.float32),
            pltpu.VMEM((2 * members, 128), jnp.float32),
            pltpu.VMEM((batch, kinds * columns // 2 * 8, 128), jnp.float32),
            pltpu.VMEM((batch // 2, members, 128), jnp.float32),
            pltpu.VMEM(fields.shape, jnp.float32),
            pltpu.SemaphoreType.DMA((kinds * columns,)),
        ],
        compiler_params=pltpu.CompilerParams(vmem_limit_bytes=24 << 20),
    )(fields, table, extras, entries, counts)


def local(prior_members, obs_column, obs_value, obs_precision, obs_list, patch_count):
    members, fields, levels, width_x, width_y = prior_members.shape
    state, table, extras = forecast(
        prior_members.reshape(members, fields * levels, width_x, width_y),
        obs_column[0], obs_value[0], obs_precision[0],
    )
    batch = obs_list.shape[0] * obs_list.shape[1]
    result = analyse(
        state,
        table,
        extras,
        obs_list.reshape(batch, obs_list.shape[2]),
        patch_count,
        width_x,
        width_y,
    )
    return result.reshape(prior_members.shape)


def solution(mesh):
    return jax.shard_map(
        local,
        mesh=mesh,
        in_specs=(
            P(None, None, None, "gx", "gy"),
            P("gx", "gy", None),
            P("gx", "gy", None),
            P("gx", "gy", None),
            P("gx", "gy", None),
            P("gx", "gy"),
        ),
        out_specs=P(None, None, None, "gx", "gy"),
        check_vma=False,
    )
```

```python
import functools

import jax
import jax.numpy as jnp
from jax import lax
from jax.experimental import pallas as pl
from jax.experimental.pallas import tpu as pltpu
from jax.sharding import PartitionSpec as P

TILE_WIDTH_CELLS = 8
STEPS = 3
NS_ITERS = 3


courant = 0.3


def split(x):
    hi = x.astype(jnp.bfloat16)
    return hi, (x - hi.astype(jnp.float32)).astype(jnp.bfloat16)


def dot_nn(a, b):
    return lax.dot_general(a, b, (((1,), (0,)), ((), ())), preferred_element_type=jnp.float32)


def dot_nt(a, b):
    return lax.dot_general(a, b, (((1,), (1,)), ((), ())), preferred_element_type=jnp.float32)


NEIGHBOURS = [(x, y) for x in (-1, 0, 1) for y in (-1, 0, 1) if (x, y) != (0, 0)]
CHUNKS = 4


def fluxes(q):
    depth, east, north = q
    height = 1.0 + depth
    inverse = 1.0 / height
    pressure = 0.5 * height * height
    speed = east * inverse
    cross = speed * north
    flux_x = (east, east * speed + pressure, cross)
    flux_y = (north, cross, north * north * inverse + pressure)
    quarter = [0.25 * v for v in q]
    flux_x = [0.5 * courant * f for f in flux_x]
    flux_y = [0.5 * courant * f for f in flux_y]
    return (
        [v - f for v, f in zip(quarter, flux_x)],
        [v + f for v, f in zip(quarter, flux_x)],
        [v - f for v, f in zip(quarter, flux_y)],
        [v + f for v, f in zip(quarter, flux_y)],
    )


def forecast_kernel(
    rows_in_x, rows_in_y, prior_ref, column_ref, value_ref, precision_ref,
    state_ref, table_out, extras_out,
    main, strips, dense_north, dense_south, north_strips, south_strips, inserts, table,
    extras, column_vmem, info_sem, load_sem, halo_send, halo_recv, strip_send, strip_recv, obs_send, obs_recv,
    extra_send, extra_recv,
):
    members, kinds, columns, lanes = prior_ref.shape
    levels = kinds // 3
    slots = column_ref.shape[1]
    pad = STEPS
    wide = columns + 2 * pad
    me_x, me_y = lax.axis_index("gx"), lax.axis_index("gy")

    def there(dx, dy):
        return {"gx": lax.rem(me_x + dx + rows_in_x, rows_in_x), "gy": me_y + dy}

    def exists(dy):
        return (me_y + dy >= 0) & (me_y + dy < rows_in_y)

    def each(act):
        for dx, dy in NEIGHBOURS:
            if dy == 0:
                act(dx, dy)
            else:
                pl.when(exists(dy))(functools.partial(act, dx, dy))

    loads = []
    for column in [*range(columns - pad, columns), *range(columns - pad)]:
        for kind in range(kinds):
            loads.append(
                pltpu.make_async_copy(
                    prior_ref.at[:, kind, column, :], main.at[kind, pad + column],
                    load_sem.at[kind, column],
                )
            )
            loads[-1].start()
    for index, (source, target) in enumerate(
        (
            (column_ref, column_vmem),
            (value_ref, extras.at[4, 0:1]),
            (precision_ref, extras.at[4, 1:2]),
        )
    ):
        loads.append(pltpu.make_async_copy(source, target, info_sem.at[index]))
        loads[-1].start()

    barrier = pltpu.get_barrier_semaphore()

    def greet(dx, dy):
        pl.semaphore_signal(barrier, 1, device_id=there(dx, dy))

    each(greet)
    sides = exists(-1).astype(jnp.int32) + exists(1).astype(jnp.int32)
    pl.semaphore_wait(barrier, 2 + 3 * sides)

    for load in loads:
        load.wait()

    def span(chunk):
        size = members // CHUNKS
        return pl.ds(chunk * size, size)

    def halo(side, chunk):
        start, stop = (columns, 0) if side == 0 else (pad, pad + columns)
        return pltpu.make_async_remote_copy(
            main.at[:, pl.ds(start, pad), span(chunk), :],
            main.at[:, pl.ds(stop, pad), span(chunk), :],
            halo_send.at[side, chunk], halo_recv.at[side, chunk],
            device_id=there(1 - 2 * side, 0),
        )

    def mirrored(dx, dy):
        return (1 - dx) * 3 + 1 - dy

    def seen(dx, dy):
        return (1 + dx) * 3 + 1 + dy

    def strip_copy(dx, dy, device):
        start = {1: columns, 0: pad, -1: pad}[dx]
        stop = {1: 0, 0: pad, -1: pad + columns}[dx]
        count = columns if dx == 0 else pad
        target = {1: south_strips, 0: strips, -1: north_strips}[dy]
        source = {1: dense_north, 0: strips, -1: dense_south}[dy]
        start = start if dy == 0 else start - pad
        return pltpu.make_async_remote_copy(
            source.at[:, pl.ds(start, count)], target.at[:, pl.ds(stop, count)],
            strip_send.at[seen(dx, dy)], strip_recv.at[mirrored(dx, dy)],
            device_id=device,
        )

    def table_copy(ref, send, recv, dx, dy, device):
        return pltpu.make_async_remote_copy(
            ref.at[4], ref.at[mirrored(dx, dy)],
            send.at[seen(dx, dy)], recv.at[mirrored(dx, dy)], device_id=device,
        )

    for side in range(2):
        halo(side, 0).start()

    lane = lax.broadcasted_iota(jnp.int32, (8, lanes), 1)
    groups = members // 8
    width = lanes // groups
    half = width // 4
    group_lane = lane % width

    def pack(kind, carry):
        raw = jnp.zeros((columns, 8, lanes), jnp.float32)
        for group in range(groups):
            part = main[kind, pad : pad + columns, 8 * group : 8 * group + 8, :]
            base = group * width
            moved = pltpu.roll(part, base + half, 2)
            raw = jnp.where(((lane >= base) & (lane < base + width))[None], moved, raw)
        strips[kind, pad : pad + columns] = jnp.where(
            (group_lane < half)[None], raw, pltpu.roll(raw, 2 * half, 2)
        )
        return carry

    lax.fori_loop(0, kinds, pack, 0)
    for level in range(levels):
        for dense, place in ((dense_north, 0), (dense_south, 3)):
            tile = None
            for field in range(3):
                piece = strips[field * levels + level, pad : pad + columns]
                shift = (field - place) * half % lanes
                piece = pltpu.roll(piece, shift, 2) if shift else piece
                tile = piece if field == 0 else jnp.where(
                    (group_lane // half == field)[None], piece, tile
                )
            dense[level] = tile
    each(lambda dx, dy: strip_copy(dx, dy, there(dx, dy)).start())

    where = column_vmem[...]
    extras[4, 2:3, :] = lax.div(where, lanes).astype(jnp.float32)
    extras[4, 3:4, :] = lax.rem(where, lanes).astype(jnp.float32)
    extras[4, 4:8, :] = jnp.zeros((4, slots), jnp.float32)
    each(lambda dx, dy: table_copy(extras, extra_send, extra_recv, dx, dy, there(dx, dy)).start())
    for chunk in range(1, CHUNKS):
        for side in range(2):
            halo(side, chunk).start()

    each(lambda dx, dy: strip_copy(-dx, -dy, there(dx, dy)).wait_recv())

    has_north = jnp.where(exists(1), 1.0, 0.0)
    has_south = jnp.where(exists(-1), 1.0, 0.0)
    own = (group_lane < half) | (group_lane >= 3 * half)
    northern = group_lane < 2 * half

    def inside(v):
        kept = jnp.where(northern, has_north, has_south) > 0.5
        return jnp.where((own | kept)[None], v, 0.0)

    for level in range(levels):
        q = []
        for field in range(3):
            kind = field * levels + level
            beyond = jnp.where(
                northern[None],
                pltpu.roll(north_strips[level], (1 - field) * half % lanes, 2),
                pltpu.roll(south_strips[level], (2 - field) * half % lanes, 2),
            )
            q.append(inside(jnp.where(own[None], strips[kind], beyond)))
        for step in range(STEPS):
            east, west, north, south = fluxes(q)
            rows = q[0].shape[0]
            fresh = []
            for field in range(3):
                up, down = north[field][1 : rows - 1], south[field][1 : rows - 1]
                inserts[step, field * levels + level, 0 : rows - 2] = jnp.where(
                    (group_lane == half)[None], up, pltpu.roll(down, lanes - 2 * half + 2, 2)
                )
                fresh.append(
                    inside(
                        east[field][2:]
                        + west[field][: rows - 2]
                        + pltpu.roll(up, lanes - 1, 2)
                        + pltpu.roll(down, 1, 2)
                    )
                )
            q = fresh

    def advance(index, carry):
        group, level = index // levels, index % levels
        part = pl.ds(pl.multiple_of(group * 8, 8), 8)
        turn = lax.rem(2 * lanes - 1 - half - group * width, lanes)
        q = [main[field * levels + level, :, part, :] for field in range(3)]
        for step in range(STEPS):
            east, west, north, south = fluxes(q)
            rows = q[0].shape[0]
            fresh = []
            for field in range(3):
                edge = pltpu.roll(inserts[step, field * levels + level, 0 : rows - 2], turn, 2)
                up = pltpu.roll(north[field][1 : rows - 1], lanes - 1, 2)
                down = pltpu.roll(south[field][1 : rows - 1], 1, 2)
                fresh.append(
                    east[field][2:]
                    + west[field][: rows - 2]
                    + jnp.where((lane == lanes - 1)[None], edge, up)
                    + jnp.where((lane == 0)[None], edge, down)
                )
            q = fresh
        for field in range(3):
            state_ref[field * levels + level, :, part, :] = q[field]
        return carry

    per_chunk = groups // CHUNKS * levels
    for chunk in range(CHUNKS):
        for side in range(2):
            halo(side, chunk).wait_recv()
        lax.fori_loop(chunk * per_chunk, (chunk + 1) * per_chunk, advance, 0)

    cell = lax.broadcasted_iota(jnp.int32, (lanes, slots), 0)
    observed = jnp.zeros((3 * members, slots), jnp.float32)
    for column in range(columns):
        layers = state_ref[0, column]
        for level in range(1, levels):
            layers = layers + state_ref[level, column]
        layers = layers / levels
        first, rest = split(layers)
        second = layers - first.astype(jnp.float32) - rest.astype(jnp.float32)
        stacked = jnp.concatenate([first, rest, second.astype(jnp.bfloat16)], axis=0)
        chosen = (cell + column * lanes == where).astype(jnp.float32).astype(jnp.bfloat16)
        observed += dot_nn(stacked, chosen)
    table[4] = observed[:members] + observed[members : 2 * members] + observed[2 * members :]
    each(lambda dx, dy: table_copy(table, obs_send, obs_recv, dx, dy, there(dx, dy)).start())

    table_out[4] = table[4]
    extras_out[4] = extras[4]

    def receive(dx, dy):
        for ref, send, recv, out in (
            (extras, extra_send, extra_recv, extras_out),
            (table, obs_send, obs_recv, table_out),
        ):
            table_copy(ref, send, recv, -dx, -dy, there(dx, dy)).wait_recv()
            out[seen(dx, dy)] = ref[seen(dx, dy)]

    each(receive)
    for chunk in range(CHUNKS):
        for side in range(2):
            halo(side, chunk).wait_send()

    def sent(dx, dy):
        strip_copy(dx, dy, there(dx, dy)).wait_send()
        table_copy(extras, extra_send, extra_recv, dx, dy, there(dx, dy)).wait_send()
        table_copy(table, obs_send, obs_recv, dx, dy, there(dx, dy)).wait_send()

    each(sent)


def forecast(prior, obs_column, obs_value, obs_precision):
    members, kinds, columns, lanes = prior.shape
    slots = obs_column.shape[1]
    wide = columns + 2 * STEPS
    vmem = pl.BlockSpec(memory_space=pltpu.VMEM)
    return pl.pallas_call(
        functools.partial(forecast_kernel, lax.axis_size("gx"), lax.axis_size("gy")),
        out_shape=(
            jax.ShapeDtypeStruct((kinds, columns, members, lanes), jnp.float32),
            jax.ShapeDtypeStruct((9, members, slots), jnp.float32),
            jax.ShapeDtypeStruct((9, 8, slots), jnp.float32),
        ),
        in_specs=[pl.BlockSpec(memory_space=pltpu.HBM)] * 4,
        out_specs=(vmem, vmem, vmem),
        scratch_shapes=[
            pltpu.VMEM((kinds, wide, members, lanes), jnp.float32),
            pltpu.VMEM((kinds, wide, 8, lanes), jnp.float32),
            pltpu.VMEM((kinds // 3, columns, 8, lanes), jnp.float32),
            pltpu.VMEM((kinds // 3, columns, 8, lanes), jnp.float32),
            pltpu.VMEM((kinds // 3, wide, 8, lanes), jnp.float32),
            pltpu.VMEM((kinds // 3, wide, 8, lanes), jnp.float32),
            pltpu.VMEM((STEPS, kinds, wide, 8, lanes), jnp.float32),
            pltpu.VMEM((9, members, slots), jnp.float32),
            pltpu.VMEM((9, 8, slots), jnp.float32),
            pltpu.VMEM((1, slots), jnp.int32),
            pltpu.SemaphoreType.DMA((3,)),
            pltpu.SemaphoreType.DMA((kinds, columns)),
            pltpu.SemaphoreType.DMA((2, CHUNKS)),
            pltpu.SemaphoreType.DMA((2, CHUNKS)),
        ]
        + [pltpu.SemaphoreType.DMA((9,))] * 6,
        compiler_params=pltpu.CompilerParams(
            collective_id=0, has_side_effects=True, vmem_limit_bytes=24 << 20
        ),
    )(*(pltpu.with_memory_space_constraint(x, pltpu.HBM) for x in (
        prior, obs_column, obs_value, obs_precision
    )))


def analysis_kernel(
    geometry, fields_ref, table_ref, extras_ref, list_ref, count_ref, out_ref,
    weights, gram, force, turned, combined, result_ref, done_sem,
):
    width_x, width_y, patches_x, patches_y, rows_in_y = geometry
    kinds, columns, members, lanes = fields_ref.shape
    tiles, _, slots = extras_ref.shape
    batch, capacity = list_ref.shape
    per_tile = slots // 128
    halves = kinds * columns // 2

    chunks = tiles * per_tile
    padded_chunks = -(-chunks // 8) * 8
    usable_at = lax.broadcasted_iota(jnp.int32, (1, capacity), 1)
    chunk_id = lax.broadcasted_iota(jnp.int32, (padded_chunks, capacity), 0)
    lane_id = lax.broadcasted_iota(jnp.int32, (128, capacity), 0)
    for patch in range(batch):
        named = list_ref[patch : patch + 1, :]
        usable = usable_at < count_ref[patch // patches_y, patch % patches_y]
        upper = jnp.where(usable, named // 128, -1)
        lower = named % 128
        counts = dot_nt(
            (chunk_id == upper).astype(jnp.float32).astype(jnp.bfloat16),
            (lane_id == lower).astype(jnp.float32).astype(jnp.bfloat16),
        )
        for chunk in range(chunks):
            tile, part = divmod(chunk, per_tile)
            weights[tile, patch : patch + 1, part * 128 : part * 128 + 128] = counts[
                chunk : chunk + 1
            ]

    patch_id = lax.broadcasted_iota(jnp.int32, (batch, slots), 0)
    centre_x = (patch_id // patches_y * TILE_WIDTH_CELLS).astype(jnp.float32) + (
        TILE_WIDTH_CELLS - 1
    ) * 0.5
    centre_y = (patch_id % patches_y * TILE_WIDTH_CELLS).astype(jnp.float32) + (
        TILE_WIDTH_CELLS - 1
    ) * 0.5
    gram[...] = jnp.zeros_like(gram)
    force[...] = jnp.zeros_like(force)
    for tile in range(tiles):
        shift_x, shift_y = tile // 3 - 1, tile % 3 - 1

        def add_tile():
            info = extras_ref[tile]
            offset_x = shift_x * width_x + info[2:3] - centre_x
            offset_y = shift_y * width_y + info[3:4] - centre_y
            near = jnp.exp(-((offset_x / width_x) ** 2) - (offset_y / width_y) ** 2)
            factor = weights[tile] * info[1:2] * near
            values = table_ref[tile]
            mean = jnp.sum(values, axis=0, keepdims=True) / members
            pert = values - mean
            upper, lower = split(pert)
            both = jnp.concatenate([upper, lower], axis=0)
            for patch in range(batch):
                first, second = split(pert * factor[patch : patch + 1])
                gram[patch] += dot_nt(jnp.concatenate([first, second], axis=0), both)
            first, second = split(factor * (info[0:1] - mean))
            rest = jnp.zeros((128 - 2 * batch, slots), jnp.bfloat16)
            force[...] += dot_nt(both, jnp.concatenate([first, second, rest], axis=0))

        row = lax.axis_index("gy") + shift_y
        pl.when((row >= 0) & (row < rows_in_y))(add_tile)

    for half in range(halves):
        kind, column = divmod(2 * half, columns)
        pair = []
        for step in range(2):
            block = fields_ref[kind, column + step]
            pair.append(block - jnp.sum(block, axis=0, keepdims=True) / members)
        flipped = jnp.transpose(jnp.concatenate(pair, axis=0))
        for strip in range(patches_y):
            turned[strip, half * 8 : half * 8 + 8, :] = flipped[strip * 8 : strip * 8 + 8]

    ahead = 256 // members
    groups = batch // ahead
    lane128 = lax.broadcasted_iota(jnp.int32, (members, 128), 1)
    own_row = lax.broadcasted_iota(jnp.int32, (members, 128), 0)
    diagonal = lane128 % members == own_row
    on_left = lane128 < members
    identity1 = jnp.where(diagonal, 1.0, 0.0)
    identity = jnp.concatenate([identity1, identity1], axis=1)
    in_block = (
        lax.broadcasted_iota(jnp.int32, (256, 256), 0) // members
        == lax.broadcasted_iota(jnp.int32, (256, 256), 1) // members
    ).astype(jnp.float32).astype(jnp.bfloat16)

    def tiled(part):
        return jnp.concatenate([part] * ahead, axis=0) * in_block

    def left(x):
        hi, lo = split(x)
        return jnp.concatenate([hi, lo], axis=0), hi

    def right(x):
        hi, lo = split(x)
        return tiled(hi), tiled(lo)

    def product(x, y):
        both = dot_nn(x[0], y[0])
        return both[:members] + both[members:] + dot_nn(x[1], y[1])

    scaled, inverse_bounds = [], []
    for group in range(groups):
        parts, bounds = [], []
        for pair in range(ahead // 2):
            even = gram[group * ahead + 2 * pair]
            odd = gram[group * ahead + 2 * pair + 1]
            matrix = jnp.where(
                on_left,
                even[:members] + pltpu.roll(even[:members], members, 1) + even[members:],
                odd[:members]
                + pltpu.roll(odd[:members], members, 1)
                + pltpu.roll(odd[members:], members, 1),
            )
            trace = jnp.where(diagonal, matrix, 0.0)
            first = jnp.sum(jnp.where(on_left, trace, 0.0), keepdims=True)
            second = jnp.sum(jnp.where(on_left, 0.0, trace), keepdims=True)
            bounds.append(members - 1.0 + jnp.where(on_left[:1], first, second))
            parts.append(matrix)
        bounds = jnp.concatenate(bounds, axis=1)
        matrix = jnp.concatenate(parts, axis=1)
        scaled.append((matrix + (members - 1.0) * identity) / bounds)
        inverse_bounds.append(1.0 / bounds)

    iterate = [left(a) for a in scaled]
    values = scaled
    factors = [1.5 * identity - 0.5 * a for a in scaled]
    roots = factors
    for repeat in range(1, NS_ITERS):
        factor_right = [right(s) for s in factors]
        iterate = [left(v) for v in values]
        values = [product(y, s) for y, s in zip(iterate, factor_right)]
        root_left = [left(z) for z in roots]
        value_right = [right(v) for v in values]
        factors = [
            1.5 * identity - 0.5 * product(z, y) for z, y in zip(root_left, value_right)
        ]
        factor_left = [left(s) for s in factors]
        root_right = [right(z) for z in roots]
        roots = [product(s, z) for s, z in zip(factor_left, root_right)]

    total = force[...]
    forcing = (
        total[:members] + pltpu.roll(total[:members], 128 - batch, 1) + total[members:]
    )
    block_row = lax.broadcasted_iota(jnp.int32, (256, 128), 0) // members
    block_lane = lax.broadcasted_iota(jnp.int32, (256, 128), 1)
    for group in range(groups):
        root = left(roots[group])
        keep = (block_row + group * ahead == block_lane).astype(jnp.float32).astype(jnp.bfloat16)
        vector = forcing
        for repeat in range(2):
            hi, lo = split(vector)
            hi = jnp.concatenate([hi] * ahead, axis=0) * keep
            lo = jnp.concatenate([lo] * ahead, axis=0) * keep
            vector = product(root, (hi, lo))
        shift = []
        for pair in range(ahead // 2):
            first = group * ahead + 2 * pair
            shift.append(
                jnp.where(on_left, vector[:, first : first + 1], vector[:, first + 1 : first + 2])
            )
        shift = jnp.concatenate(shift, axis=1)
        inverse = inverse_bounds[group]
        whole = jnp.sqrt((members - 1.0) * inverse) * roots[group] + shift * inverse
        for pair in range(ahead // 2):
            combined[group * (ahead // 2) + pair] = whole[:, pair * 128 : pair * 128 + 128]

    for strip in range(batch):
        both = combined[strip // 2]
        other = pltpu.roll(both, members, 1)
        on_diag, off_diag = (both, other) if strip % 2 == 0 else (other, both)
        matrix = jnp.concatenate(
            [jnp.where(on_left, on_diag, 0.0), jnp.where(on_left, 0.0, off_diag)], axis=0
        )
        hi, lo = split(matrix)
        upper, lower = split(turned[strip])
        turned[strip] = dot_nn(
            jnp.concatenate([upper, lower], axis=1), jnp.concatenate([hi, hi], axis=0)
        ) + dot_nn(upper, lo)

    copies = []
    for half in range(halves):
        kind, column = divmod(2 * half, columns)
        result = jnp.transpose(
            jnp.concatenate(
                [turned[strip, half * 8 : half * 8 + 8, :] for strip in range(patches_y)], axis=0
            )
        )
        for step in range(2):
            block = fields_ref[kind, column + step]
            mean = jnp.sum(block, axis=0, keepdims=True) / members
            result_ref[kind, column + step] = (
                mean + result[step * members : step * members + members]
            )
            copies.append(
                pltpu.make_async_copy(
                    result_ref.at[kind, column + step],
                    out_ref.at[:, kind, column + step, :],
                    done_sem.at[kind * columns + column + step],
                )
            )
            copies[-1].start()
    for copy in copies:
        copy.wait()


def analyse(fields, table, extras, entries, counts, width_x, width_y):
    kinds, columns, members, lanes = fields.shape
    tiles, _, slots = extras.shape
    batch = entries.shape[0]
    geometry = (
        width_x, width_y, width_x // TILE_WIDTH_CELLS, width_y // TILE_WIDTH_CELLS,
        lax.axis_size("gy"),
    )
    vmem = pl.BlockSpec(memory_space=pltpu.VMEM)
    return pl.pallas_call(
        functools.partial(analysis_kernel, geometry),
        out_shape=jax.ShapeDtypeStruct((members, kinds, columns, lanes), jnp.float32),
        in_specs=[vmem] * 4 + [pl.BlockSpec(memory_space=pltpu.SMEM)],
        out_specs=pl.BlockSpec(memory_space=pl.ANY),
        scratch_shapes=[
            pltpu.VMEM((tiles, batch, slots), jnp.float32),
            pltpu.VMEM((batch, 2 * members, 2 * members), jnp.float32),
            pltpu.VMEM((2 * members, 128), jnp.float32),
            pltpu.VMEM((batch, kinds * columns // 2 * 8, 128), jnp.float32),
            pltpu.VMEM((batch // 2, members, 128), jnp.float32),
            pltpu.VMEM(fields.shape, jnp.float32),
            pltpu.SemaphoreType.DMA((kinds * columns,)),
        ],
        compiler_params=pltpu.CompilerParams(vmem_limit_bytes=24 << 20),
    )(fields, table, extras, entries, counts)


def local(prior_members, obs_column, obs_value, obs_precision, obs_list, patch_count):
    members, fields, levels, width_x, width_y = prior_members.shape
    state, table, extras = forecast(
        prior_members.reshape(members, fields * levels, width_x, width_y),
        obs_column[0], obs_value[0], obs_precision[0],
    )
    batch = obs_list.shape[0] * obs_list.shape[1]
    result = analyse(
        state,
        table,
        extras,
        obs_list.reshape(batch, obs_list.shape[2]),
        patch_count,
        width_x,
        width_y,
    )
    return result.reshape(prior_members.shape)


def solution(mesh):
    return jax.shard_map(
        local,
        mesh=mesh,
        in_specs=(
            P(None, None, None, "gx", "gy"),
            P("gx", "gy", None),
            P("gx", "gy", None),
            P("gx", "gy", None),
            P("gx", "gy", None),
            P("gx", "gy"),
        ),
        out_specs=P(None, None, None, "gx", "gy"),
        check_vma=False,
    )
```
